512 devices in a mesh: grid: 64 (over y, z), member: 8 (over x, core).
Axes of the slice: x: 4, y: 4, z: 16, core: 2. Of those that a mesh axis runs over, the one named last changes fastest.
Arguments:
- state_ens: float32 [1024, 32, 128], P('grid', 'member'), may hold values from -6 to 6
- obs_ens: float32 [8192, 32, 128], P('grid', 'member'), may hold values from -6 to 6
- obs_value: float32 [8192, 128], P('grid'), may hold values from -8 to 8
- obs_rinv: float32 [8192, 128], P('grid'), may hold values from 0.25 to 4
- loc_weight: float32 [1024, 8, 8], P('grid'), may hold values from 0.05 to 1
- pair_block: int32 [1024, 8], P('grid'), may hold values from 0 to 383, as said below
- pair_count: int32 [1024], P('grid'), may hold values from 4 to 8, as said below
Outputs:
- analysis_ens: float32 [1024, 32, 128], P('grid', 'member')
The draws below stay inside these ranges and needn't reach their ends.
Inputs may be any that keep to these rules, and one draw needn't show every extreme that they name: `pair_block`: pairs of a state block lie near its place within the slab, reaching into the neighbouring slabs; the first pair of every state block is in use. `pair_count`: the first state block of every slab uses all 8 pairs.
All inputs are finite; a program needn't handle non-finite values.
Results may differ from the reference program's by a relative error of at most 0.00017.
Values sent between devices are 32-bit elements; how exact they have to be, the bound alone decides.
No kernel may reach another device: no remote copies, remote signals or barrier semaphores. Data moves between devices by JAX's collectives and lax.ppermute only.
A program may use at most 64 MiB of HBM per device.

```python
import math
import jax
import jax.numpy as jnp
from jax import lax

K = 32
BV = 128
OBS = 128
Q = 8
P_SIZE = 8
NS = 7
SB = 16
OB = 128
NSB = 1024
NOB = 8192
N_GRID = 64


def draw_pair_block(key, part):
    rows = jnp.arange(NSB, dtype=jnp.int32)
    local = rows % SB
    center = OB + local * OB // SB + OB // (2 * SB)
    offset = jax.random.randint(jax.random.fold_in(key, 11), (NSB, P_SIZE), -OB, OB + 1, dtype=jnp.int32)
    picked = jnp.clip(center[:, None] + offset, 0, 3 * OB - 1)
    first = jnp.where(local == 0, 0, jnp.where(local == SB - 1, 3 * OB - 1, picked[:, 0]))
    return picked.at[:, 0].set(first).astype(jnp.int32)


def draw_pair_count(key, part):
    rows = jnp.arange(NSB, dtype=jnp.int32)
    counts = jax.random.randint(jax.random.fold_in(key, 23), (NSB,), P_SIZE // 2, P_SIZE + 1, dtype=jnp.int32)
    return jnp.where(rows % SB == 0, P_SIZE, counts).astype(jnp.int32)


def level_of(key, shape, split, least, largest):
    factor_of = 1.0
    for dim, shards_of in split:
        steps = jax.random.uniform(jax.random.fold_in(jax.random.fold_in(key, 6), dim), (shards_of,), jnp.float32, least / len(split), largest / len(split))
        factor_of = factor_of * jnp.repeat(jnp.exp(steps), shape[dim] // shards_of).reshape((-1,) + (1,) * (len(shape) - 1 - dim))
    return factor_of


def gaussian(stream_key, dims, scale, reach, split=(), held_as=jnp.bfloat16):
    array = jax.random.normal(stream_key, dims, jnp.float32) * scale
    if len(split) > 0:
        array = level_of(stream_key, dims, split, -0.22, 0.18) * array
    return jnp.clip(array, min=-reach, max=reach).astype(held_as)


def setup_inputs(seed: int = 0) -> dict:
    seeds = jax.random.split(jax.random.key(seed), 8)
    state_ens = gaussian(seeds[0], (NSB, K, BV), 1.0, 6.0, ((0, 64), (1, 8)), jnp.float32)
    obs_ens = gaussian(seeds[1], (NOB, K, OBS), 1.0, 6.0, ((0, 64), (1, 8)), jnp.float32)
    obs_value = gaussian(seeds[2], (NOB, OBS), 1.5, 8.0, ((0, 64),), jnp.float32)
    obs_rinv = jnp.clip(jnp.exp(math.log(4.0) - 2.7725887 * jax.random.uniform(seeds[3], (NOB, OBS), jnp.float32) ** level_of(seeds[3], (NOB, OBS), ((0, 64),), -0.2, 0.2)), 0.25, 4.0)
    loc_weight = jnp.clip(jnp.exp(math.log(1.0) - 2.9957323 * jax.random.uniform(seeds[4], (NSB, Q, P_SIZE), jnp.float32) ** level_of(seeds[4], (NSB, Q, P_SIZE), ((0, 64),), -0.2, 0.2)), 0.05, 1.0)
    pair_block = draw_pair_block(jax.random.fold_in(seeds[7], 71), 0)
    pair_count = draw_pair_count(jax.random.fold_in(seeds[7], 71), 0)
    return {"state_ens": state_ens, "obs_ens": obs_ens, "obs_value": obs_value, "obs_rinv": obs_rinv, "loc_weight": loc_weight, "pair_block": pair_block, "pair_count": pair_count}


def transform(combo, members):
    precise = lax.Precision.HIGHEST
    identity = jnp.eye(members, dtype=jnp.float32)
    shape_lead = combo.shape[:-1]
    amat = combo[..., :members * members].reshape(shape_lead + (members, members)) + (members - 1.0) * identity
    drive = combo[..., members * members:]
    frobenius = jnp.sqrt(lax.optimization_barrier(jnp.sum(amat * amat, axis=(-2, -1), keepdims=True)))
    root_part = amat / frobenius
    inverse_part = jnp.broadcast_to(identity, amat.shape)
    for iterate in range(NS):
        middle = 1.5 * identity - 0.5 * jnp.einsum('...ij,...jk->...ik', inverse_part, root_part, precision=precise)
        root_part = jnp.einsum('...ij,...jk->...ik', root_part, middle, precision=precise)
        inverse_part = jnp.einsum('...ij,...jk->...ik', middle, inverse_part, precision=precise)
    inverse = jnp.einsum('...ij,...jk->...ik', inverse_part, inverse_part, precision=precise) / frobenius
    wmean = jnp.einsum('...ij,...j->...i', inverse, drive, precision=precise)
    return jnp.sqrt(members - 1.0) * inverse_part / jnp.sqrt(frobenius) + wmean[..., :, None]

def obs_terms(ensemble, values, weights):
    precise = lax.Precision.HIGHEST
    ymean = lax.optimization_barrier(jnp.mean(ensemble, axis=1))
    perturb = ensemble - ymean[:, None, :]
    innovation = values - ymean
    weighted = perturb * weights[:, None, :]
    grams = jnp.einsum('bko,bmo->bkm', weighted, perturb, precision=precise)
    vector = jnp.einsum('bko,bo->bk', weighted, innovation, precision=precise)
    return jnp.concatenate([grams.reshape(grams.shape[0], -1), vector], axis=1)

def reference(state_ens, obs_ens, obs_value, obs_rinv, loc_weight, pair_block, pair_count):
    precise = lax.Precision.HIGHEST
    ordered = jnp.swapaxes(obs_ens.reshape(N_GRID, OB, K, OBS), 0, 1).reshape(NOB, K, OBS)
    values = jnp.swapaxes(obs_value.reshape(N_GRID, OB, OBS), 0, 1).reshape(NOB, OBS)
    weights = jnp.swapaxes(obs_rinv.reshape(N_GRID, OB, OBS), 0, 1).reshape(NOB, OBS)
    packed = obs_terms(ordered, values, weights)
    slabs = jnp.arange(NSB, dtype=jnp.int32) // SB
    target = (slabs[:, None] * OB + pair_block - OB).astype(jnp.int32)
    inside = ((target >= 0) & (target < NOB)).astype(jnp.float32)
    chosen = packed[jnp.clip(target, 0, NOB - 1)] * inside[..., None]
    live = (jnp.arange(P_SIZE, dtype=jnp.int32)[None, :] < pair_count[:, None]).astype(jnp.float32)
    weight = loc_weight * live[:, None, :]
    combo = jnp.einsum('sqp,spc->sqc', weight, chosen, precision=precise)
    trans = transform(combo, K)
    update = jnp.einsum('smqv,sqmk->skqv', state_ens.reshape(NSB, K, Q, BV // Q), trans, precision=precise)
    return update.reshape(NSB, K, BV)
```

```python
import functools

import jax
import jax.numpy as jnp
from jax import lax
from jax.experimental import pallas as pl
from jax.experimental.pallas import tpu as pltpu
from jax.sharding import PartitionSpec as P

K = 32
BV = 128
Q = 8
P_SIZE = 8
NS = 7
SB = 16
OB = 128
MEMBERS = 8
GRID = 64
LANES = 128
F32 = jnp.float32
HIGHEST = lax.Precision.HIGHEST
INTERPRET = False
VMEM_BYTES = 8 << 20


def iota(shape, dim):
    return lax.broadcasted_iota(jnp.int32, shape, dim)


def slot_mask(row, column):
    return column == jnp.bitwise_and(row + 8, K - 1)


def call(kernel, out_rows, *args, smem=()):
    specs = [
        pl.BlockSpec(memory_space=pltpu.SMEM if i in smem else pltpu.VMEM)
        for i in range(len(args))
    ]
    return pl.pallas_call(
        kernel,
        out_shape=jax.ShapeDtypeStruct((out_rows, LANES), F32),
        in_specs=specs,
        out_specs=pl.BlockSpec(memory_space=pltpu.VMEM),
        compiler_params=pltpu.CompilerParams(vmem_limit_bytes=VMEM_BYTES),
        interpret=INTERPRET,
        name=kernel.__name__,
    )(*args)


def terms_kernel(member_ref, ens_ref, value_ref, rinv_ref, out_ref):
    start = pl.multiple_of(member_ref[0] * 16, 16)
    values = value_ref[pl.ds(start, 16), :]
    weights = rinv_ref[pl.ds(start, 16), :]
    part = iota((8, LANES), 1) // K
    column = jnp.bitwise_and(iota((8, LANES), 1), K - 1)
    slot = slot_mask(part * 8 + iota((8, LANES), 0), column)
    for row in range(16):
        tiles = [ens_ref[pl.ds(row * 4 + kk, 8, stride=64), :] for kk in range(4)]
        ensemble = jnp.concatenate(tiles, axis=0)
        mean = jnp.sum(ensemble, axis=0, keepdims=True) * (1.0 / K)
        perturb = ensemble - mean
        innovation = values[row : row + 1, :] - mean
        weighted = perturb * weights[row : row + 1, :]
        gram = lax.dot_general(
            weighted,
            jnp.concatenate([perturb] * 4, axis=0),
            (((1,), (1,)), ((), ())),
            precision=HIGHEST,
            preferred_element_type=F32,
        )
        vector = jnp.sum(weighted * innovation, axis=1, keepdims=True)
        terms = gram[0:8]
        vecs = jnp.broadcast_to(vector[0:8], (8, LANES))
        for kk in range(1, 4):
            here = part == kk
            terms = jnp.where(here, gram[kk * 8 : kk * 8 + 8], terms)
            vecs = jnp.where(here, vector[kk * 8 : kk * 8 + 8], vecs)
        out_ref[pl.ds(row, 8, stride=16), :] = jnp.where(slot, vecs, terms)


def window_kernel(in_ref, out_ref):
    for jb in range(2):
        rows = in_ref[pl.ds(jb, GRID, stride=2), :]
        out_ref[pl.ds(2 + jb, GRID, stride=6), :] = rows
        out_ref[pl.ds(jb, GRID, stride=6), :] = pltpu.roll(rows, 1, 0)
        out_ref[pl.ds(4 + jb, GRID, stride=6), :] = pltpu.roll(rows, GRID - 1, 0)


def combine_kernel(grid_ref, in_ref, weight_ref, block_ref, count_ref, state_ref, out_ref, combo_ref):
    slab = grid_ref[0]
    row = iota((6 * GRID, 1), 0)
    where = row // 6
    block = (row - where * 6) * GRID + where
    target = slab * OB + block - OB
    inside = jnp.logical_and(target >= 0, target < GRID * OB)
    block = jnp.where(inside, block, -1)
    picked = jnp.concatenate([block_ref[...]] * Q, axis=1)
    weight = jnp.concatenate([weight_ref[q] for q in range(Q)], axis=1)
    count = jnp.concatenate([count_ref[...]] * Q, axis=1)
    live = iota((P_SIZE, LANES), 0) < count
    weight = jnp.where(live, weight, 0.0)
    mix = jnp.zeros((6 * GRID, LANES), F32)
    for p in range(P_SIZE):
        mix = mix + jnp.where(block == picked[p : p + 1], weight[p : p + 1], 0.0)
    combo_ref[...] = lax.dot_general(
        mix,
        in_ref[...],
        (((0,), (0,)), ((), ())),
        precision=HIGHEST,
        preferred_element_type=F32,
    )
    for q in range(Q):
        for s0 in range(2):
            out_ref[pl.ds(q * 2 + s0, 8, stride=24), :] = combo_ref[pl.ds(q * 16 + s0, 8, stride=2), :]
    for r in range(8):
        out_ref[pl.ds(16 + r, 8, stride=24), :] = state_ref[pl.ds(r, 8, stride=8), :]


def spread(flat, mask):
    return jnp.where(mask, jnp.concatenate([flat] * 8, axis=0), 0.0)


def product(left, right):
    return jnp.dot(left, right, precision=HIGHEST, preferred_element_type=F32)


def transform_kernel(in_ref, out_ref):
    width = Q * K
    mask = iota((width, width), 0) // K == iota((width, width), 1) // K
    ones = mask.astype(F32)
    part = iota((8, LANES), 1) // K
    row = iota((K, width), 0)
    column = jnp.bitwise_and(iota((K, width), 1), K - 1)
    slot = slot_mask(row, column)
    identity = (row == column).astype(F32)
    slab_v = iota((K, LANES), 1) // (BV // Q)
    for s0 in range(2):
        tiles = [in_ref[pl.ds(q * 2 + s0, 8, stride=24), :] for q in range(Q)]
        rows = []
        for kk in range(4):
            halves = []
            for half in range(2):
                acc = None
                for qq in range(4):
                    tile = tiles[half * 4 + qq]
                    shift = (qq - kk) * K % LANES
                    if shift:
                        tile = pltpu.roll(tile, shift, 1)
                    acc = tile if acc is None else jnp.where(part == qq, tile, acc)
                halves.append(acc)
            rows.append(jnp.concatenate(halves, axis=1))
        packed = jnp.concatenate(rows, axis=0)
        lifted = jnp.concatenate([packed[8:], packed[:8]], axis=0)
        mirror = jnp.where(
            column >= 8, pltpu.roll(lifted, 8, 1), pltpu.roll(lifted, width - 24, 1)
        )
        amat = jnp.where(slot, mirror, packed) + (K - 1.0) * identity
        squares = jnp.sum(amat * amat, axis=0, keepdims=True)
        sums = product(
            jnp.concatenate(
                [jnp.where(slot, packed, 0.0), jnp.broadcast_to(squares, (8, width))], axis=0
            ),
            ones,
        )
        drive = sums[:K]
        frobenius = jnp.sqrt(sums[K : K + 1])
        root = amat / frobenius
        middle = 1.5 * identity - 0.5 * root
        both = product(root, spread(middle, mask))
        root = both
        inverse = middle
        for _ in range(1, NS - 1):
            middle = 1.5 * identity - 0.5 * product(inverse, spread(root, mask))
            both = product(jnp.concatenate([root, inverse], axis=0), spread(middle, mask))
            root = both[:K]
            inverse = both[K:]
        middle = 1.5 * identity - 0.5 * product(inverse, spread(root, mask))
        inverse = product(inverse, spread(middle, mask))
        first = jnp.sum(inverse * drive, axis=0, keepdims=True)
        wmean = product(inverse * first, ones) / frobenius
        trans = jnp.sqrt(K - 1.0) * inverse / jnp.sqrt(frobenius) + wmean
        state = jnp.concatenate(
            [in_ref[pl.ds(16 + s0 * 4 + kk, 8, stride=24), :] for kk in range(4)], axis=0
        )
        full = lax.dot_general(
            trans,
            state,
            (((0,), (0,)), ((), ())),
            precision=HIGHEST,
            preferred_element_type=F32,
        )
        update = full[0:K]
        for q in range(1, Q):
            update = jnp.where(slab_v == q, full[q * K : (q + 1) * K], update)
        for kk in range(4):
            out_ref[pl.ds(s0 * 4 + kk, 8, stride=8), :] = update[kk * 8 : kk * 8 + 8]


def swap(array, axis):
    return lax.all_to_all(array, axis, split_axis=0, concat_axis=0, tiled=True)


def local(state_ens, obs_ens, obs_value, obs_rinv, loc_weight, pair_block, pair_count):
    member = lax.axis_index("member").astype(jnp.int32).reshape(1)
    slab = lax.axis_index("grid").astype(jnp.int32).reshape(1)
    gathered = swap(obs_ens.reshape(OB * 4, LANES), "member")
    terms = call(terms_kernel, OB, member, gathered, obs_value, obs_rinv, smem=(0,))
    shares = swap(terms, "member")
    windows = call(window_kernel, 6 * GRID, shares)
    arrived = swap(windows.reshape(3 * GRID, 2, LANES), "grid").reshape(6 * GRID, LANES)
    combos = pl.pallas_call(
        combine_kernel,
        out_shape=jax.ShapeDtypeStruct((8 * 24, LANES), F32),
        in_specs=[pl.BlockSpec(memory_space=pltpu.SMEM)] + [pl.BlockSpec(memory_space=pltpu.VMEM)] * 5,
        out_specs=pl.BlockSpec(memory_space=pltpu.VMEM),
        scratch_shapes=[pltpu.VMEM((LANES, LANES), F32)],
        compiler_params=pltpu.CompilerParams(vmem_limit_bytes=VMEM_BYTES),
        interpret=INTERPRET,
        name="combine_kernel",
    )(
        slab,
        arrived,
        jnp.transpose(loc_weight, (1, 2, 0)),
        jnp.transpose(pair_block, (1, 0)),
        pair_count.reshape(1, SB),
        state_ens.reshape(SB * 4, LANES),
    )
    matrices = swap(combos, "member")
    update = call(transform_kernel, SB * 4, matrices)
    return swap(update, "member").reshape(SB, 4, BV)


def solution(mesh):
    return jax.shard_map(
        local,
        mesh=mesh,
        in_specs=(
            P("grid", "member", None),
            P("grid", "member", None),
            P("grid", None),
            P("grid", None),
            P("grid", None, None),
            P("grid", None),
            P("grid"),
        ),
        out_specs=P("grid", "member", None),
        check_vma=False,
    )
```

```python
import functools

import jax
import jax.numpy as jnp
from jax import lax
from jax.experimental import pallas as pl
from jax.experimental.pallas import tpu as pltpu
from jax.sharding import PartitionSpec as P

K = 32
BV = 128
Q = 8
P_SIZE = 8
NS = 7
SB = 16
OB = 128
MEMBERS = 8
GRID = 64
LANES = 128
F32 = jnp.float32
BF16 = jnp.bfloat16
HIGHEST = lax.Precision.HIGHEST
INTERPRET = False
VMEM_BYTES = 8 << 20


def iota(shape, dim):
    return lax.broadcasted_iota(jnp.int32, shape, dim)


def slot_mask(row, column):
    return column == jnp.bitwise_and(row + 8, K - 1)


def call(kernel, out_rows, *args, scalars=0, unplaced=0, scratch=()):
    vmem = pl.BlockSpec(memory_space=pltpu.VMEM)
    placed = [vmem] * (len(args) - scalars - unplaced)
    return pl.pallas_call(
        kernel,
        out_shape=[jax.ShapeDtypeStruct((rows, LANES), F32) for rows in out_rows],
        in_specs=[pl.BlockSpec(memory_space=pltpu.SMEM)] * scalars
        + placed
        + [pl.BlockSpec(memory_space=pltpu.HBM)] * unplaced,
        out_specs=[vmem] * len(out_rows),
        scratch_shapes=scratch,
        compiler_params=pltpu.CompilerParams(vmem_limit_bytes=VMEM_BYTES),
        interpret=INTERPRET,
        name=kernel.__name__,
    )(*args)


def hold(array):
    return array if INTERPRET else pltpu.with_memory_space_constraint(array, pltpu.HBM)


def mixing(slab, weight_ref, block_ref, count_ref):
    row = iota((6 * GRID, 1), 0)
    where = row // 6
    block = (row - where * 6) * GRID + where
    target = slab * OB + block - OB
    inside = jnp.logical_and(target >= 0, target < GRID * OB)
    block = jnp.where(inside, block, -1)
    picked = jnp.concatenate([block_ref[...]] * Q, axis=1)
    weight = jnp.concatenate([weight_ref[q] for q in range(Q)], axis=1)
    count = jnp.concatenate([count_ref[...]] * Q, axis=1)
    live = iota((P_SIZE, LANES), 0) < count
    weight = jnp.where(live, weight, 0.0)
    mix = jnp.zeros((6 * GRID, LANES), F32)
    for p in range(P_SIZE):
        mix = mix + jnp.where(block == picked[p : p + 1], weight[p : p + 1], 0.0)
    return mix


def terms_kernel(
    slab_ref,
    member_ref,
    ens_ref,
    value_ref,
    rinv_ref,
    weight_ref,
    block_hbm,
    count_hbm,
    out_ref,
    mix_ref,
    block_ref,
    count_ref,
    sems,
):
    fetches = [
        pltpu.make_async_copy(block_hbm, block_ref, sems.at[0]),
        pltpu.make_async_copy(count_hbm, count_ref, sems.at[1]),
    ]
    for fetch in fetches:
        fetch.start()
    start = pl.multiple_of(member_ref[0] * 16, 16)
    values = value_ref[pl.ds(start, 16), :]
    weights = rinv_ref[pl.ds(start, 16), :]
    part = iota((8, LANES), 1) // K
    column = jnp.bitwise_and(iota((8, LANES), 1), K - 1)
    slot = slot_mask(part * 8 + iota((8, LANES), 0), column)
    for row in range(16):
        tiles = [ens_ref[pl.ds(row * 4 + kk, 8, stride=64), :] for kk in range(4)]
        ensemble = jnp.concatenate(tiles, axis=0)
        mean = jnp.sum(ensemble, axis=0, keepdims=True) * (1.0 / K)
        perturb = ensemble - mean
        innovation = values[row : row + 1, :] - mean
        weighted = perturb * weights[row : row + 1, :]
        gram = lax.dot_general(
            weighted,
            jnp.concatenate([perturb] * 4, axis=0),
            (((1,), (1,)), ((), ())),
            precision=HIGHEST,
            preferred_element_type=F32,
        )
        vector = jnp.sum(weighted * innovation, axis=1, keepdims=True)
        terms = gram[0:8]
        vecs = jnp.broadcast_to(vector[0:8], (8, LANES))
        for kk in range(1, 4):
            here = part == kk
            terms = jnp.where(here, gram[kk * 8 : kk * 8 + 8], terms)
            vecs = jnp.where(here, vector[kk * 8 : kk * 8 + 8], vecs)
        out_ref[pl.ds(row, 8, stride=16), :] = jnp.where(slot, vecs, terms)
    for fetch in fetches:
        fetch.wait()
    mix_ref[...] = mixing(slab_ref[0], weight_ref, block_ref, count_ref)


def window_kernel(in_ref, out_ref):
    for jb in range(2):
        rows = in_ref[pl.ds(jb, GRID, stride=2), :]
        out_ref[pl.ds(2 + jb, GRID, stride=6), :] = rows
        out_ref[pl.ds(jb, GRID, stride=6), :] = pltpu.roll(rows, 1, 0)
        out_ref[pl.ds(4 + jb, GRID, stride=6), :] = pltpu.roll(rows, GRID - 1, 0)


def combine_kernel(in_ref, mix_ref, state_ref, out_ref, combo_ref):
    combo_ref[...] = lax.dot_general(
        mix_ref[...],
        in_ref[...],
        (((0,), (0,)), ((), ())),
        precision=HIGHEST,
        preferred_element_type=F32,
    )
    for q in range(Q):
        for s0 in range(2):
            out_ref[pl.ds(q * 2 + s0, 8, stride=24), :] = combo_ref[pl.ds(q * 16 + s0, 8, stride=2), :]
    for r in range(8):
        out_ref[pl.ds(16 + r, 8, stride=24), :] = state_ref[pl.ds(r, 8, stride=8), :]


def halves(value):
    high = value.astype(BF16)
    return high, (value - high.astype(F32)).astype(BF16)


def dot(left, right):
    return jnp.dot(left, right, preferred_element_type=F32)


def product(left, right, ones):
    high, low = halves(left)
    right_high, right_low = (jnp.concatenate([half] * Q, axis=0) * ones for half in halves(right))
    rows = left.shape[0]
    wide = dot(jnp.concatenate([high, low], axis=0), right_high)
    return wide[:rows] + wide[rows:] + dot(high, right_low)


def segment_sum(value, ones):
    high, rest = value.astype(BF16), value
    rest = rest - high.astype(F32)
    middle = rest.astype(BF16)
    low = (rest - middle.astype(F32)).astype(BF16)
    rows = value.shape[0]
    wide = dot(jnp.concatenate([high, middle, low], axis=0), ones)
    return wide[:rows] + wide[rows : 2 * rows] + wide[2 * rows :]


def roll_segment(value, shift, column):
    width = value.shape[1]
    return jnp.where(
        column >= shift, pltpu.roll(value, shift, 1), pltpu.roll(value, width - K + shift, 1)
    )


def transform_kernel(in_ref, out_ref):
    width = Q * K
    ones = (iota((width, width), 0) // K == iota((width, width), 1) // K).astype(F32).astype(BF16)
    part = iota((8, LANES), 1) // K
    row = iota((K, width), 0)
    column = jnp.bitwise_and(iota((K, width), 1), K - 1)
    slot = slot_mask(row, column)
    identity = (row == column).astype(F32)
    point = iota((width, BV), 0) // K == iota((width, BV), 1) // (BV // Q)
    point = point.astype(F32).astype(BF16)
    pair = range(2)
    amats, drives = [], []
    for s0 in pair:
        tiles = [in_ref[pl.ds(q * 2 + s0, 8, stride=24), :] for q in range(Q)]
        rows = []
        for kk in range(4):
            sides = []
            for half in range(2):
                acc = None
                for qq in range(4):
                    tile = tiles[half * 4 + qq]
                    shift = (qq - kk) * K % LANES
                    if shift:
                        tile = pltpu.roll(tile, shift, 1)
                    acc = tile if acc is None else jnp.where(part == qq, tile, acc)
                sides.append(acc)
            rows.append(jnp.concatenate(sides, axis=1))
        packed = jnp.concatenate(rows, axis=0)
        mirror = roll_segment(jnp.concatenate(rows[1:] + rows[:1], axis=0), 8, column)
        amats.append(jnp.where(slot, mirror, packed) + (K - 1.0) * identity)
        drive = jnp.sum(jnp.where(slot, packed, 0.0), axis=0, keepdims=True)
        drives.append(roll_segment(jnp.broadcast_to(drive, (8, width)), K - 8, column[:8])[:1])
    squares = [
        jnp.broadcast_to(jnp.sum(amat * amat, axis=0, keepdims=True), (8, width)) for amat in amats
    ]
    sums = segment_sum(jnp.concatenate(squares, axis=0), ones)
    frobenius = [jnp.sqrt(sums[8 * s0 : 8 * s0 + 1]) for s0 in pair]
    root = [amats[s0] / frobenius[s0] for s0 in pair]
    inverse = [1.5 * identity - 0.5 * root[s0] for s0 in pair]
    root = [product(root[s0], inverse[s0], ones) for s0 in pair]
    for _ in range(1, NS - 1):
        middle = [1.5 * identity - 0.5 * product(inverse[s0], root[s0], ones) for s0 in pair]
        both = [
            product(jnp.concatenate([root[s0], inverse[s0]], axis=0), middle[s0], ones) for s0 in pair
        ]
        root = [both[s0][:K] for s0 in pair]
        inverse = [both[s0][K:] for s0 in pair]
    middle = [1.5 * identity - 0.5 * product(inverse[s0], root[s0], ones) for s0 in pair]
    inverse = [product(inverse[s0], middle[s0], ones) for s0 in pair]
    first = [segment_sum(inverse[s0] * drives[s0], ones) for s0 in pair]
    for s0 in pair:
        wmean = jnp.sum(inverse[s0] * first[s0], axis=0, keepdims=True) / frobenius[s0]
        trans = inverse[s0] * (jnp.sqrt(K - 1.0) / jnp.sqrt(frobenius[s0])) + wmean
        state = jnp.concatenate(
            [in_ref[pl.ds(16 + s0 * 4 + kk, 8, stride=24), :] for kk in range(4)], axis=0
        )
        update = product(trans, state, point)
        for kk in range(4):
            out_ref[pl.ds(s0 * 4 + kk, 8, stride=8), :] = update[kk * 8 : kk * 8 + 8]


def swap(array, axis):
    return lax.all_to_all(array, axis, split_axis=0, concat_axis=0, tiled=True)


def local(state_ens, obs_ens, obs_value, obs_rinv, loc_weight, pair_block, pair_count):
    slab = lax.axis_index("grid").astype(jnp.int32).reshape(1)
    member = lax.axis_index("member").astype(jnp.int32).reshape(1)
    gathered = swap(obs_ens.reshape(OB * 4, LANES), "member")
    terms, mix = call(
        terms_kernel,
        (OB, 6 * GRID),
        slab,
        member,
        gathered,
        obs_value,
        obs_rinv,
        jnp.transpose(loc_weight, (1, 2, 0)),
        hold(jnp.transpose(pair_block, (1, 0))),
        hold(pair_count.reshape(1, SB)),
        scalars=2,
        unplaced=2,
        scratch=[
            pltpu.VMEM((P_SIZE, SB), jnp.int32),
            pltpu.VMEM((1, SB), jnp.int32),
            pltpu.SemaphoreType.DMA((2,)),
        ],
    )
    shares = swap(terms, "member")
    (windows,) = call(window_kernel, (6 * GRID,), shares)
    arrived = swap(windows.reshape(3 * GRID, 2, LANES), "grid").reshape(6 * GRID, LANES)
    (combos,) = call(
        combine_kernel,
        (8 * 24,),
        arrived,
        mix,
        state_ens.reshape(SB * 4, LANES),
        scratch=[pltpu.VMEM((LANES, LANES), F32)],
    )
    matrices = swap(combos, "member")
    (update,) = call(transform_kernel, (SB * 4,), matrices)
    return swap(update.reshape(SB, 4, BV), "member")


def solution(mesh):
    return jax.shard_map(
        local,
        mesh=mesh,
        in_specs=(
            P("grid", "member", None),
            P("grid", "member", None),
            P("grid", None),
            P("grid", None),
            P("grid", None, None),
            P("grid", None),
            P("grid"),
        ),
        out_specs=P("grid", "member", None),
        check_vma=False,
    )
```

```python
import functools

import jax
import jax.numpy as jnp
from jax import lax
from jax.experimental import pallas as pl
from jax.experimental.pallas import tpu as pltpu
from jax.sharding import PartitionSpec as P

K = 32
BV = 128
Q = 8
P_SIZE = 8
NS = 7
SB = 16
OB = 128
MEMBERS = 8
GRID = 64
LANES = 128
F32 = jnp.float32
BF16 = jnp.bfloat16
HIGHEST = lax.Precision.HIGHEST
INTERPRET = False
VMEM_BYTES = 8 << 20

START = (0, 32, 56, 72)


def iota(shape, dim):
    return lax.broadcasted_iota(jnp.int32, shape, dim)


def low3(value):
    return jnp.bitwise_and(value, 7)


def halves(value):
    high = value.astype(BF16)
    return high, (value - high.astype(F32)).astype(BF16)


def dot(left, right):
    return jnp.dot(left, right, preferred_element_type=F32)


def dot_rows(left, right):
    return lax.dot_general(left, right, (((1,), (1,)), ((), ())), preferred_element_type=F32)


def call(kernel, out_rows, *args, scalars=0, unplaced=0, scratch=()):
    vmem = pl.BlockSpec(memory_space=pltpu.VMEM)
    placed = [vmem] * (len(args) - scalars - unplaced)
    return pl.pallas_call(
        kernel,
        out_shape=[jax.ShapeDtypeStruct((rows, LANES), F32) for rows in out_rows],
        in_specs=[pl.BlockSpec(memory_space=pltpu.SMEM)] * scalars
        + placed
        + [pl.BlockSpec(memory_space=pltpu.HBM)] * unplaced,
        out_specs=[vmem] * len(out_rows),
        scratch_shapes=scratch,
        compiler_params=pltpu.CompilerParams(vmem_limit_bytes=VMEM_BYTES),
        interpret=INTERPRET,
        name=kernel.__name__,
    )(*args)


def hold(array):
    return array if INTERPRET else pltpu.with_memory_space_constraint(array, pltpu.HBM)


def mixing(slab, weight_ref, block_ref, count_ref, mix_ref):
    picked = jnp.concatenate([block_ref[...]] * Q, axis=1)
    weight = jnp.concatenate([weight_ref[q] for q in range(Q)], axis=1)
    count = jnp.concatenate([count_ref[...]] * Q, axis=1)
    target = slab * OB + picked - OB
    used = jnp.logical_and(target >= 0, target < GRID * OB)
    used = jnp.logical_and(used, iota((P_SIZE, LANES), 0) < count)
    weight = jnp.where(used, weight, 0.0)
    step = 16
    block = iota((step, LANES), 0)
    for first in range(0, 3 * OB, step):
        mix = jnp.zeros((step, LANES), F32)
        for p in range(P_SIZE):
            mix = mix + jnp.where(block + first == picked[p : p + 1], weight[p : p + 1], 0.0)
        mix_ref[first : first + step] = mix


def terms_kernel(
    slab_ref,
    member_ref,
    ens_ref,
    value_ref,
    rinv_ref,
    weight_ref,
    block_hbm,
    count_hbm,
    out_ref,
    mix_ref,
    block_ref,
    count_ref,
    sems,
):
    fetches = [
        pltpu.make_async_copy(block_hbm, block_ref, sems.at[0]),
        pltpu.make_async_copy(count_hbm, count_ref, sems.at[1]),
    ]
    for fetch in fetches:
        fetch.start()
    start = pl.multiple_of(member_ref[0] * 16, 16)
    values = value_ref[pl.ds(start, 16), :]
    weights = rinv_ref[pl.ds(start, 16), :]
    lane = iota((8, LANES), 1)
    share = iota((8, LANES), 0)
    for four in range(4):
        perturbs, weighteds, vectors = [], [], []
        for row in range(four * 4, four * 4 + 4):
            tiles = [ens_ref[pl.ds(row * 4 + kk, 8, stride=64), :] for kk in range(4)]
            ensemble = jnp.concatenate(tiles, axis=0)
            mean = jnp.sum(ensemble, axis=0, keepdims=True) * (1.0 / K)
            perturb = ensemble - mean
            weighted = perturb * weights[row : row + 1, :]
            innovation = values[row : row + 1, :] - mean
            vectors.append(jnp.sum(weighted * innovation, axis=1, keepdims=True))
            perturbs.append(perturb)
            weighteds.append(weighted)
        high, low = halves(jnp.concatenate(weighteds, axis=0))
        right_high, right_low = halves(jnp.concatenate(perturbs, axis=0))
        grams = dot_rows(
            jnp.concatenate([high, low], axis=1), jnp.concatenate([right_high, right_high], axis=1)
        ) + dot_rows(high, right_low)
        terms = []
        for j in range(4):
            acc = None
            for kk in range(4):
                tile = grams[j * K + kk * 8 : j * K + kk * 8 + 8]
                shift = (START[kk] - kk * 8 - j * K) % LANES
                if shift:
                    tile = pltpu.roll(tile, shift, 1)
                slot = lane == START[kk] + low3(share + 1)
                tile = jnp.where(slot, vectors[j][kk * 8 : kk * 8 + 8], tile)
                acc = tile if acc is None else jnp.where(lane >= START[kk], tile, acc)
            terms.append(acc)
        for j in range(2):
            even = terms[2 * j]
            odd = pltpu.roll(terms[2 * j + 1], 64, 1)
            main = jnp.where(lane < 64, even, odd)
            rest = jnp.where(lane < 16, pltpu.roll(even, 64, 1), pltpu.roll(odd, 16, 1))
            out_ref[pl.ds(four * 2 + j, 8, stride=16), :] = main
            out_ref[pl.ds(8 + four * 2 + j, 8, stride=16), :] = rest
    for fetch in fetches:
        fetch.wait()
    mixing(slab_ref[0], weight_ref, block_ref, count_ref, mix_ref)


def window_kernel(in_ref, out_ref):
    main = jnp.concatenate([in_ref[m * 16 : m * 16 + 8] for m in range(8)], axis=0)
    rest = jnp.concatenate([in_ref[m * 16 + 8 : m * 16 + 16] for m in range(8)], axis=0)
    lane = iota((GRID, LANES), 1)
    out_ref[pl.ds(0, GRID, stride=4), :] = pltpu.roll(main, 1, 0)
    out_ref[pl.ds(1, GRID, stride=4), :] = main
    out_ref[pl.ds(2, GRID, stride=4), :] = pltpu.roll(main, GRID - 1, 0)
    before = pltpu.roll(rest, 1, 0)
    after = pltpu.roll(pltpu.roll(rest, GRID - 1, 0), 64, 1)
    here = pltpu.roll(rest, 32, 1)
    out_ref[pl.ds(3, GRID, stride=4), :] = jnp.where(
        lane < 32, before, jnp.where(lane < 64, here, after)
    )


def combine_kernel(in_ref, mix_ref, state_ref, out_ref, combo_ref):
    lane = iota((GRID, LANES), 1)
    rest = in_ref[pl.ds(3, GRID, stride=4), :]
    rows = []
    for d in range(3):
        main = in_ref[pl.ds(d, GRID, stride=4), :]
        for jb in range(2):
            first = pltpu.roll(main, 64, 1) if jb else main
            shift = (64 - d * 32 - jb * 16) % LANES
            last = pltpu.roll(rest, shift, 1) if shift else rest
            rows.append(jnp.where(lane < 64, first, last))
    combo_ref[...] = lax.dot_general(
        mix_ref[...],
        jnp.concatenate(rows, axis=0),
        (((0,), (0,)), ((), ())),
        precision=HIGHEST,
        preferred_element_type=F32,
    )
    for q in range(Q):
        for s0 in range(2):
            out_ref[pl.ds(q * 2 + s0, 8, stride=24), :] = combo_ref[pl.ds(q * 16 + s0, 8, stride=2), :]
    for r in range(8):
        out_ref[pl.ds(16 + r, 8, stride=24), :] = state_ref[pl.ds(r, 8, stride=8), :]


def product(left, right, ones):
    high, low = halves(left)
    right_high, right_low = (jnp.concatenate([half] * Q, axis=0) * ones for half in halves(right))
    rows = left.shape[0]
    wide = dot(jnp.concatenate([high, low], axis=0), right_high)
    return wide[:rows] + wide[rows:] + dot(high, right_low)


def thirds(value):
    high = value.astype(BF16)
    rest = value - high.astype(F32)
    middle = rest.astype(BF16)
    return high, middle, (rest - middle.astype(F32)).astype(BF16)


def segment_sum(value, ones):
    rows = value.shape[0]
    wide = dot(jnp.concatenate(thirds(value), axis=0), ones)
    return wide[:rows] + wide[rows : 2 * rows] + wide[2 * rows :]


def mirrored(value, identity, ones):
    total = 0.0
    for third in thirds(value)[::-1]:
        total = total + dot_rows(identity, jnp.concatenate([third] * Q, axis=0) * ones)
    return total


def transform_kernel(in_ref, out_ref):
    width = Q * K
    ones = (iota((width, width), 0) // K == iota((width, width), 1) // K).astype(F32).astype(BF16)
    lane = iota((8, LANES), 1)
    row = iota((K, width), 0)
    column = jnp.bitwise_and(iota((K, width), 1), K - 1)
    diagonal = row // 8 == column // 8
    slot = jnp.logical_and(diagonal, low3(column) == low3(row + 1))
    keep = jnp.logical_or(row // 8 < column // 8, jnp.logical_and(diagonal, jnp.logical_not(slot)))
    identity = (row == column).astype(F32)
    point = iota((width, BV), 0) // K == iota((width, BV), 1) // (BV // Q)
    point = point.astype(F32).astype(BF16)
    pair = range(2)
    amats, drives = [], []
    for s0 in pair:
        tiles = [in_ref[pl.ds(q * 2 + s0, 8, stride=24), :] for q in range(Q)]
        rows = []
        for kk in range(4):
            sides = []
            for half in range(2):
                acc = jnp.zeros((8, LANES), F32)
                for qq in range(4):
                    tile = tiles[half * 4 + qq]
                    shift = (qq * K + kk * 8 - START[kk]) % LANES
                    if shift:
                        tile = pltpu.roll(tile, shift, 1)
                    inside = jnp.logical_and(lane >= qq * K + kk * 8, lane < qq * K + K)
                    acc = jnp.where(inside, tile, acc)
                sides.append(acc)
            rows.append(jnp.concatenate(sides, axis=1))
        packed = jnp.concatenate(rows, axis=0)
        flipped = mirrored(packed, identity.astype(BF16), ones)
        amats.append(jnp.where(keep, packed, flipped) + (K - 1.0) * identity)
        drive = jnp.sum(jnp.where(slot, packed, 0.0), axis=0, keepdims=True)
        drive = jnp.broadcast_to(drive, (8, width))
        drive = jnp.where(
            low3(column[:8]) == 7, pltpu.roll(drive, 7, 1), pltpu.roll(drive, width - 1, 1)
        )
        drives.append(drive[:1])
    squares = [
        jnp.broadcast_to(jnp.sum(amat * amat, axis=0, keepdims=True), (8, width)) for amat in amats
    ]
    sums = segment_sum(jnp.concatenate(squares, axis=0), ones)
    frobenius = [jnp.sqrt(sums[8 * s0 : 8 * s0 + 1]) for s0 in pair]
    root = [amats[s0] / frobenius[s0] for s0 in pair]
    inverse = [1.5 * identity - 0.5 * root[s0] for s0 in pair]
    root = [product(root[s0], inverse[s0], ones) for s0 in pair]
    for _ in range(1, NS - 1):
        middle = [1.5 * identity - 0.5 * product(inverse[s0], root[s0], ones) for s0 in pair]
        both = [
            product(jnp.concatenate([root[s0], inverse[s0]], axis=0), middle[s0], ones) for s0 in pair
        ]
        root = [both[s0][:K] for s0 in pair]
        inverse = [both[s0][K:] for s0 in pair]
    middle = [1.5 * identity - 0.5 * product(inverse[s0], root[s0], ones) for s0 in pair]
    inverse = [product(inverse[s0], middle[s0], ones) for s0 in pair]
    first = [segment_sum(inverse[s0] * drives[s0], ones) for s0 in pair]
    for s0 in pair:
        wmean = jnp.sum(inverse[s0] * first[s0], axis=0, keepdims=True) / frobenius[s0]
        trans = inverse[s0] * (jnp.sqrt(K - 1.0) / jnp.sqrt(frobenius[s0])) + wmean
        state = jnp.concatenate(
            [in_ref[pl.ds(16 + s0 * 4 + kk, 8, stride=24), :] for kk in range(4)], axis=0
        )
        update = product(trans, state, point)
        for kk in range(4):
            out_ref[pl.ds(s0 * 4 + kk, 8, stride=8), :] = update[kk * 8 : kk * 8 + 8]


def swap(array, axis):
    return lax.all_to_all(array, axis, split_axis=0, concat_axis=0, tiled=True)


def local(state_ens, obs_ens, obs_value, obs_rinv, loc_weight, pair_block, pair_count):
    slab = lax.axis_index("grid").astype(jnp.int32).reshape(1)
    member = lax.axis_index("member").astype(jnp.int32).reshape(1)
    gathered = swap(obs_ens.reshape(OB * 4, LANES), "member")
    terms, mix = call(
        terms_kernel,
        (OB, 3 * OB),
        slab,
        member,
        gathered,
        obs_value,
        obs_rinv,
        jnp.transpose(loc_weight, (1, 2, 0)),
        hold(jnp.transpose(pair_block, (1, 0))),
        hold(pair_count.reshape(1, SB)),
        scalars=2,
        unplaced=2,
        scratch=[
            pltpu.VMEM((P_SIZE, SB), jnp.int32),
            pltpu.VMEM((1, SB), jnp.int32),
            pltpu.SemaphoreType.DMA((2,)),
        ],
    )
    shares = swap(terms, "member")
    (windows,) = call(window_kernel, (4 * GRID,), shares)
    arrived = swap(windows.reshape(GRID, 4, LANES), "grid").reshape(4 * GRID, LANES)
    (combos,) = call(
        combine_kernel,
        (8 * 24,),
        arrived,
        mix,
        state_ens.reshape(SB * 4, LANES),
        scratch=[pltpu.VMEM((LANES, LANES), F32)],
    )
    matrices = swap(combos, "member")
    (update,) = call(transform_kernel, (SB * 4,), matrices)
    return swap(update.reshape(SB, 4, BV), "member")


def solution(mesh):
    return jax.shard_map(
        local,
        mesh=mesh,
        in_specs=(
            P("grid", "member", None),
            P("grid", "member", None),
            P("grid", None),
            P("grid", None),
            P("grid", None, None),
            P("grid", None),
            P("grid"),
        ),
        out_specs=P("grid", "member", None),
        check_vma=False,
    )
```

```python
import functools

import jax
import jax.numpy as jnp
from jax import lax
from jax.experimental import pallas as pl
from jax.experimental.pallas import tpu as pltpu
from jax.sharding import PartitionSpec as P

K = 32
BV = 128
Q = 8
P_SIZE = 8
NS = 7
SB = 16
OB = 128
MEMBERS = 8
GRID = 64
LANES = 128
F32 = jnp.float32
BF16 = jnp.bfloat16
HIGHEST = lax.Precision.HIGHEST
INTERPRET = False
VMEM_BYTES = 8 << 20

START = (0, 32, 56, 72)


def iota(shape, dim):
    return lax.broadcasted_iota(jnp.int32, shape, dim)


def low3(value):
    return jnp.bitwise_and(value, 7)


def halves(value):
    high = value.astype(BF16)
    return high, (value - high.astype(F32)).astype(BF16)


def dot(left, right):
    return jnp.dot(left, right, preferred_element_type=F32)


def dot_rows(left, right):
    return lax.dot_general(left, right, (((1,), (1,)), ((), ())), preferred_element_type=F32)


def call(kernel, outs, *args, scalars=0, unplaced=0, scratch=()):
    vmem = pl.BlockSpec(memory_space=pltpu.VMEM)
    return pl.pallas_call(
        kernel,
        out_shape=[
            out if isinstance(out, jax.ShapeDtypeStruct) else jax.ShapeDtypeStruct((out, LANES), F32)
            for out in outs
        ],
        in_specs=[pl.BlockSpec(memory_space=pltpu.SMEM)] * scalars
        + [vmem] * (len(args) - scalars - unplaced)
        + [pl.BlockSpec(memory_space=pl.ANY)] * unplaced,
        out_specs=[vmem] * len(outs),
        scratch_shapes=scratch,
        compiler_params=pltpu.CompilerParams(vmem_limit_bytes=VMEM_BYTES),
        interpret=INTERPRET,
        name=kernel.__name__,
    )(*args)


def mix_kernel(slab_ref, weight_ref, block_ref, count_ref, out_ref, mix_ref):
    picked = jnp.concatenate([block_ref[...]] * Q, axis=1)
    weight = jnp.concatenate([weight_ref[q] for q in range(Q)], axis=1)
    count = jnp.concatenate([count_ref[...]] * Q, axis=1)
    target = slab_ref[0] * OB + picked - OB
    used = jnp.logical_and(target >= 0, target < GRID * OB)
    used = jnp.logical_and(used, iota((P_SIZE, LANES), 0) < count)
    weight = jnp.where(used, weight, 0.0)
    step = 16
    block = iota((step, LANES), 0)
    for first in range(0, 3 * OB, step):
        mix = jnp.zeros((step, LANES), F32)
        for p in range(P_SIZE):
            mix = mix + jnp.where(block + first == picked[p : p + 1], weight[p : p + 1], 0.0)
        mix_ref[first : first + step] = mix
    out_ref[...] = jnp.concatenate(halves(jnp.transpose(mix_ref[...])), axis=1)


def terms_kernel(member_ref, ens_ref, value_ref, rinv_ref, _, out_ref):
    start = pl.multiple_of(member_ref[0] * 16, 16)
    values = value_ref[pl.ds(start, 16), :]
    weights = rinv_ref[pl.ds(start, 16), :]
    lane = iota((8, LANES), 1)
    share = iota((8, LANES), 0)
    for four in range(4):
        perturbs, weighteds, vectors = [], [], []
        for row in range(four * 4, four * 4 + 4):
            tiles = [ens_ref[pl.ds(row * 4 + kk, 8, stride=64), :] for kk in range(4)]
            ensemble = jnp.concatenate(tiles, axis=0)
            mean = jnp.sum(ensemble, axis=0, keepdims=True) * (1.0 / K)
            perturb = ensemble - mean
            weighted = perturb * weights[row : row + 1, :]
            innovation = values[row : row + 1, :] - mean
            vectors.append(jnp.sum(weighted * innovation, axis=1, keepdims=True))
            perturbs.append(perturb)
            weighteds.append(weighted)
        high, low = halves(jnp.concatenate(weighteds, axis=0))
        right_high, right_low = halves(jnp.concatenate(perturbs, axis=0))
        grams = dot_rows(
            jnp.concatenate([high, low], axis=1), jnp.concatenate([right_high, right_high], axis=1)
        ) + dot_rows(high, right_low)
        terms = []
        for j in range(4):
            acc = None
            for kk in range(4):
                tile = grams[j * K + kk * 8 : j * K + kk * 8 + 8]
                shift = (START[kk] - kk * 8 - j * K) % LANES
                if shift:
                    tile = pltpu.roll(tile, shift, 1)
                slot = lane == START[kk] + low3(share + 1)
                tile = jnp.where(slot, vectors[j][kk * 8 : kk * 8 + 8], tile)
                acc = tile if acc is None else jnp.where(lane >= START[kk], tile, acc)
            terms.append(acc)
        for j in range(2):
            even = terms[2 * j]
            odd = pltpu.roll(terms[2 * j + 1], 64, 1)
            main = jnp.where(lane < 64, even, odd)
            rest = jnp.where(lane < 16, pltpu.roll(even, 64, 1), pltpu.roll(odd, 16, 1))
            out_ref[pl.ds(four * 2 + j, 8, stride=16), :] = main
            out_ref[pl.ds(8 + four * 2 + j, 8, stride=16), :] = rest


def window_kernel(in_ref, out_ref):
    main = jnp.concatenate([in_ref[m * 16 : m * 16 + 8] for m in range(8)], axis=0)
    rest = jnp.concatenate([in_ref[m * 16 + 8 : m * 16 + 16] for m in range(8)], axis=0)
    lane = iota((GRID, LANES), 1)
    out_ref[pl.ds(0, GRID, stride=4), :] = pltpu.roll(main, 1, 0)
    out_ref[pl.ds(1, GRID, stride=4), :] = main
    out_ref[pl.ds(2, GRID, stride=4), :] = pltpu.roll(main, GRID - 1, 0)
    before = pltpu.roll(rest, 1, 0)
    after = pltpu.roll(pltpu.roll(rest, GRID - 1, 0), 64, 1)
    here = pltpu.roll(rest, 32, 1)
    out_ref[pl.ds(3, GRID, stride=4), :] = jnp.where(
        lane < 32, before, jnp.where(lane < 64, here, after)
    )


def combine_kernel(in_ref, mix_ref, state_ref, out_ref, combo_ref):
    lane = iota((GRID, LANES), 1)
    rest = in_ref[pl.ds(3, GRID, stride=4), :]
    rows = []
    for d in range(3):
        main = in_ref[pl.ds(d, GRID, stride=4), :]
        for jb in range(2):
            first = pltpu.roll(main, 64, 1) if jb else main
            shift = (64 - d * 32 - jb * 16) % LANES
            last = pltpu.roll(rest, shift, 1) if shift else rest
            rows.append(jnp.where(lane < 64, first, last))
    high, low = halves(jnp.concatenate(rows, axis=0))
    mix = mix_ref[...]
    combo_ref[...] = dot(mix, jnp.concatenate([high, high], axis=0)) + dot(mix[:, : 3 * OB], low)
    for q in range(Q):
        for s0 in range(2):
            out_ref[pl.ds(q * 2 + s0, 8, stride=24), :] = combo_ref[pl.ds(q * 16 + s0, 8, stride=2), :]
    for r in range(8):
        out_ref[pl.ds(16 + r, 8, stride=24), :] = state_ref[pl.ds(r, 8, stride=8), :]


def spread(value, mask):
    blocks = mask.shape[0] // value.shape[0]
    return jnp.concatenate(
        [jnp.concatenate([half] * blocks, axis=0) * mask for half in halves(value)], axis=1
    )


def product(left, right):
    columns = right.shape[1] // 2
    high, low = halves(left)
    return dot(
        jnp.concatenate([high, low], axis=1),
        jnp.concatenate([right[:, :columns]] * 2, axis=0),
    ) + dot(high, right[:, columns:])


def thirds(value):
    high = value.astype(BF16)
    rest = value - high.astype(F32)
    middle = rest.astype(BF16)
    return high, middle, (rest - middle.astype(F32)).astype(BF16)


def segment_sum(value, ones):
    rows = value.shape[0]
    wide = dot(jnp.concatenate(thirds(value), axis=0), ones)
    return wide[:rows] + wide[rows : 2 * rows] + wide[2 * rows :]


def mirrored(value, identity, ones):
    high, middle, low = [jnp.concatenate([third] * 4, axis=0) * ones for third in thirds(value)]
    return dot_rows(
        jnp.concatenate([identity] * 2, axis=1), jnp.concatenate([high, middle], axis=1)
    ) + dot_rows(identity, low)


def transform_kernel(in_ref, out_ref):
    def same(shape, rows, lanes):
        return (iota(shape, 0) // rows == iota(shape, 1) // lanes).astype(F32).astype(BF16)

    ones = same((LANES, LANES), K, K)
    point = same((Q * K, BV), K, BV // Q)
    lane = iota((8, LANES), 1)
    row = iota((K, LANES), 0)
    column = jnp.bitwise_and(iota((K, LANES), 1), K - 1)
    diagonal = row // 8 == column // 8
    slot = jnp.logical_and(diagonal, low3(column) == low3(row + 1))
    keep = jnp.logical_or(row // 8 < column // 8, jnp.logical_and(diagonal, jnp.logical_not(slot)))
    identity = (row == column).astype(F32)
    mirror = jnp.logical_and(diagonal, low3(row) == low3(column + 1))
    times = jnp.where(diagonal, jnp.where(slot, 0.0, jnp.where(mirror, 2.0, 1.0)), 2.0)
    groups = range(4)
    amats, drives, squares = [], [], []
    for g in groups:
        tiles = [in_ref[pl.ds((g % 2 * 4 + qq) * 2 + g // 2, 8, stride=24), :] for qq in range(4)]
        rows = []
        for kk in range(4):
            acc = jnp.zeros((8, LANES), F32)
            for qq in range(4):
                tile = tiles[qq]
                shift = (qq * K + kk * 8 - START[kk]) % LANES
                if shift:
                    tile = pltpu.roll(tile, shift, 1)
                inside = jnp.logical_and(lane >= qq * K + kk * 8, lane < qq * K + K)
                acc = jnp.where(inside, tile, acc)
            rows.append(acc)
        packed = jnp.concatenate(rows, axis=0)
        flipped = mirrored(packed, identity.astype(BF16), ones)
        amats.append(jnp.where(keep, packed, flipped) + (K - 1.0) * identity)
        square = packed + (K - 1.0) * identity
        square = jnp.sum(square * square * times, axis=0, keepdims=True)
        squares.append(jnp.broadcast_to(square, (8, LANES)))
        drive = jnp.sum(jnp.where(slot, packed, 0.0), axis=0, keepdims=True)
        drive = jnp.broadcast_to(drive, (8, LANES))
        drive = jnp.where(low3(lane) == 7, pltpu.roll(drive, 7, 1), pltpu.roll(drive, LANES - 1, 1))
        drives.append(drive[:1])
    sums = segment_sum(jnp.concatenate(squares, axis=0), ones)
    frobenius = [jnp.sqrt(sums[8 * g : 8 * g + 1]) for g in groups]
    root = [amats[g] / frobenius[g] for g in groups]
    inverse = [1.5 * identity - 0.5 * root[g] for g in groups]
    for step in range(NS - 1):
        blocks = [spread(root[g], ones) for g in groups]
        if step == 0:
            square = [product(root[g], blocks[g]) for g in groups]
        else:
            square = [product(root[g], blocks[g]) for g in groups]
            inverse = [1.5 * inverse[g] - 0.5 * product(inverse[g], blocks[g]) for g in groups]
        middle = [2.25 * identity - 1.5 * root[g] + 0.25 * square[g] for g in groups]
        root = [product(middle[g], blocks[g]) for g in groups]
    blocks = [spread(root[g], ones) for g in groups]
    inverse = [1.5 * inverse[g] - 0.5 * product(inverse[g], blocks[g]) for g in groups]
    for s0 in range(2):
        both = slice(2 * s0, 2 * s0 + 2)
        wide = jnp.concatenate(inverse[both], axis=1)
        state = jnp.concatenate(
            [in_ref[pl.ds(16 + s0 * 4 + kk, 8, stride=24), :] for kk in range(4)], axis=0
        )
        moved = product(wide, spread(state, point))
        first = segment_sum(wide * jnp.concatenate(drives[both], axis=1), point)
        norm = jnp.sqrt(segment_sum(jnp.concatenate(squares[both], axis=1), point)[:1])
        shift = jnp.sum(first * moved, axis=0, keepdims=True) / norm
        update = moved * (jnp.sqrt(K - 1.0) / jnp.sqrt(norm)) + shift
        for kk in range(4):
            out_ref[pl.ds(s0 * 4 + kk, 8, stride=8), :] = update[kk * 8 : kk * 8 + 8]


def swap(array, axis):
    return lax.all_to_all(array, axis, split_axis=0, concat_axis=0, tiled=True)


def local(state_ens, obs_ens, obs_value, obs_rinv, loc_weight, pair_block, pair_count):
    slab = lax.axis_index("grid").astype(jnp.int32).reshape(1)
    member = lax.axis_index("member").astype(jnp.int32).reshape(1)
    gathered = swap(obs_ens.reshape(OB * 4, LANES), "member")
    (mix,) = call(
        mix_kernel,
        (jax.ShapeDtypeStruct((LANES, 6 * OB), BF16),),
        slab,
        jnp.transpose(loc_weight, (1, 2, 0)),
        jnp.transpose(pair_block, (1, 0)),
        pair_count.reshape(1, SB),
        scalars=1,
        scratch=[pltpu.VMEM((3 * OB, LANES), F32)],
    )
    (terms,) = call(
        terms_kernel, (OB,), member, gathered, obs_value, obs_rinv, mix, scalars=1, unplaced=1
    )
    shares = swap(terms, "member")
    (windows,) = call(window_kernel, (4 * GRID,), shares)
    arrived = swap(windows.reshape(GRID, 4, LANES), "grid").reshape(4 * GRID, LANES)
    (combos,) = call(
        combine_kernel,
        (8 * 24,),
        arrived,
        mix,
        state_ens.reshape(SB * 4, LANES),
        scratch=[pltpu.VMEM((LANES, LANES), F32)],
    )
    matrices = swap(combos, "member")
    (update,) = call(transform_kernel, (SB * 4,), matrices)
    return swap(update.reshape(SB, 4, BV), "member")


def solution(mesh):
    return jax.shard_map(
        local,
        mesh=mesh,
        in_specs=(
            P("grid", "member", None),
            P("grid", "member", None),
            P("grid", None),
            P("grid", None),
            P("grid", None, None),
            P("grid", None),
            P("grid"),
        ),
        out_specs=P("grid", "member", None),
        check_vma=False,
    )
```

```python
import functools

import jax
import jax.numpy as jnp
from jax import lax
from jax.experimental import pallas as pl
from jax.experimental.pallas import tpu as pltpu
from jax.sharding import PartitionSpec as P

K = 32
BV = 128
Q = 8
P_SIZE = 8
NS = 7
SB = 16
OB = 128
MEMBERS = 8
GRID = 64
LANES = 128
F32 = jnp.float32
BF16 = jnp.bfloat16
HIGHEST = lax.Precision.HIGHEST
INTERPRET = False
VMEM_BYTES = 8 << 20

START = (0, 32, 56, 72)


def iota(shape, dim):
    return lax.broadcasted_iota(jnp.int32, shape, dim)


def low3(value):
    return jnp.bitwise_and(value, 7)


def thirds(value):
    high = value.astype(BF16)
    rest = value - high.astype(F32)
    middle = rest.astype(BF16)
    return high, middle, (rest - middle.astype(F32)).astype(BF16)


def dot(left, right):
    return jnp.dot(left, right, preferred_element_type=F32)


def dot_rows(left, right):
    return lax.dot_general(left, right, (((1,), (1,)), ((), ())), preferred_element_type=F32)


def product(left, right, form, axis):
    high, middle, low = left
    first, second, third = right
    both = jnp.concatenate([high, middle], axis=1)
    return (
        form(both, jnp.concatenate([first] * 2, axis=axis))
        + form(both, jnp.concatenate([second] * 2, axis=axis))
        + form(jnp.concatenate([low, high], axis=1), jnp.concatenate([first, third], axis=axis))
    )


def call(kernel, outs, *args, scalars=0, unplaced=0, scratch=()):
    vmem = pl.BlockSpec(memory_space=pltpu.VMEM)
    return pl.pallas_call(
        kernel,
        out_shape=[
            out if isinstance(out, jax.ShapeDtypeStruct) else jax.ShapeDtypeStruct((out, LANES), F32)
            for out in outs
        ],
        in_specs=[pl.BlockSpec(memory_space=pltpu.SMEM)] * scalars
        + [vmem] * (len(args) - scalars - unplaced)
        + [pl.BlockSpec(memory_space=pl.ANY)] * unplaced,
        out_specs=[vmem] * len(outs),
        scratch_shapes=scratch,
        compiler_params=pltpu.CompilerParams(vmem_limit_bytes=VMEM_BYTES),
        interpret=INTERPRET,
        name=kernel.__name__,
    )(*args)


def mix_kernel(slab_ref, weight_ref, block_ref, count_ref, out_ref, mix_ref):
    picked = jnp.concatenate([block_ref[...]] * Q, axis=1)
    weight = jnp.concatenate([weight_ref[q] for q in range(Q)], axis=1)
    count = jnp.concatenate([count_ref[...]] * Q, axis=1)
    target = slab_ref[0] * OB + picked - OB
    used = jnp.logical_and(target >= 0, target < GRID * OB)
    used = jnp.logical_and(used, iota((P_SIZE, LANES), 0) < count)
    weight = jnp.where(used, weight, 0.0)
    step = 16
    block = iota((step, LANES), 0)
    for first in range(0, 3 * OB, step):
        mix = jnp.zeros((step, LANES), F32)
        for p in range(P_SIZE):
            mix = mix + jnp.where(block + first == picked[p : p + 1], weight[p : p + 1], 0.0)
        mix_ref[first : first + step] = mix
    out_ref[...] = jnp.concatenate(thirds(jnp.transpose(mix_ref[...])), axis=1)


def terms_kernel(member_ref, ens_ref, value_ref, rinv_ref, _, out_ref):
    start = pl.multiple_of(member_ref[0] * 16, 16)
    values = value_ref[pl.ds(start, 16), :]
    weights = rinv_ref[pl.ds(start, 16), :]
    lane = iota((8, LANES), 1)
    share = iota((8, LANES), 0)
    for four in range(4):
        perturbs, weighteds, vectors = [], [], []
        for row in range(four * 4, four * 4 + 4):
            tiles = [ens_ref[pl.ds(row * 4 + kk, 8, stride=64), :] for kk in range(4)]
            ensemble = jnp.concatenate(tiles, axis=0)
            mean = jnp.sum(ensemble, axis=0, keepdims=True) * (1.0 / K)
            perturb = ensemble - mean
            weighted = perturb * weights[row : row + 1, :]
            innovation = values[row : row + 1, :] - mean
            vectors.append(jnp.sum(weighted * innovation, axis=1, keepdims=True))
            perturbs.append(perturb)
            weighteds.append(weighted)
        grams = product(
            thirds(jnp.concatenate(weighteds, axis=0)),
            thirds(jnp.concatenate(perturbs, axis=0)),
            dot_rows,
            1,
        )
        terms = []
        for j in range(4):
            acc = None
            for kk in range(4):
                tile = grams[j * K + kk * 8 : j * K + kk * 8 + 8]
                shift = (START[kk] - kk * 8 - j * K) % LANES
                if shift:
                    tile = pltpu.roll(tile, shift, 1)
                slot = lane == START[kk] + low3(share + 1)
                tile = jnp.where(slot, vectors[j][kk * 8 : kk * 8 + 8], tile)
                acc = tile if acc is None else jnp.where(lane >= START[kk], tile, acc)
            terms.append(acc)
        for j in range(2):
            even = terms[2 * j]
            odd = pltpu.roll(terms[2 * j + 1], 64, 1)
            main = jnp.where(lane < 64, even, odd)
            rest = jnp.where(lane < 16, pltpu.roll(even, 64, 1), pltpu.roll(odd, 16, 1))
            out_ref[pl.ds(four * 2 + j, 8, stride=16), :] = main
            out_ref[pl.ds(8 + four * 2 + j, 8, stride=16), :] = rest


def window_kernel(in_ref, out_ref):
    main = jnp.concatenate([in_ref[m * 16 : m * 16 + 8] for m in range(8)], axis=0)
    rest = jnp.concatenate([in_ref[m * 16 + 8 : m * 16 + 16] for m in range(8)], axis=0)
    lane = iota((GRID, LANES), 1)
    out_ref[pl.ds(0, GRID, stride=4), :] = pltpu.roll(main, 1, 0)
    out_ref[pl.ds(1, GRID, stride=4), :] = main
    out_ref[pl.ds(2, GRID, stride=4), :] = pltpu.roll(main, GRID - 1, 0)
    before = pltpu.roll(rest, 1, 0)
    after = pltpu.roll(pltpu.roll(rest, GRID - 1, 0), 64, 1)
    here = pltpu.roll(rest, 32, 1)
    out_ref[pl.ds(3, GRID, stride=4), :] = jnp.where(
        lane < 32, before, jnp.where(lane < 64, here, after)
    )


def combine_kernel(in_ref, mix_ref, state_ref, out_ref, combo_ref):
    lane = iota((GRID, LANES), 1)
    rest = in_ref[pl.ds(3, GRID, stride=4), :]
    rows = []
    for d in range(3):
        main = in_ref[pl.ds(d, GRID, stride=4), :]
        for jb in range(2):
            first = pltpu.roll(main, 64, 1) if jb else main
            shift = (64 - d * 32 - jb * 16) % LANES
            last = pltpu.roll(rest, shift, 1) if shift else rest
            rows.append(jnp.where(lane < 64, first, last))
    high, middle, low = thirds(jnp.concatenate(rows, axis=0))
    mix = mix_ref[...]
    combo_ref[...] = (
        dot(mix, jnp.concatenate([high] * 3, axis=0))
        + dot(mix[:, : 6 * OB], jnp.concatenate([middle] * 2, axis=0))
        + dot(mix[:, : 3 * OB], low)
    )
    for q in range(Q):
        for s0 in range(2):
            out_ref[pl.ds(q * 2 + s0, 8, stride=24), :] = combo_ref[pl.ds(q * 16 + s0, 8, stride=2), :]
    for r in range(8):
        out_ref[pl.ds(16 + r, 8, stride=24), :] = state_ref[pl.ds(r, 8, stride=8), :]


def spread(value, mask):
    blocks = mask.shape[0] // value.shape[0]
    return [jnp.concatenate([third] * blocks, axis=0) * mask for third in thirds(value)]


def segment_sum(value, ones):
    rows = value.shape[0]
    wide = dot(jnp.concatenate(thirds(value), axis=0), ones)
    return wide[:rows] + wide[rows : 2 * rows] + wide[2 * rows :]


def mirrored(value, identity, ones):
    high, middle, low = [jnp.concatenate([third] * 4, axis=0) * ones for third in thirds(value)]
    return dot_rows(
        jnp.concatenate([identity] * 2, axis=1), jnp.concatenate([high, middle], axis=1)
    ) + dot_rows(identity, low)


def transform_kernel(in_ref, out_ref):
    def same(shape, rows, lanes):
        return (iota(shape, 0) // rows == iota(shape, 1) // lanes).astype(F32).astype(BF16)

    ones = same((LANES, LANES), K, K)
    point = same((Q * K, BV), K, BV // Q)
    lane = iota((8, LANES), 1)
    row = iota((K, LANES), 0)
    column = jnp.bitwise_and(iota((K, LANES), 1), K - 1)
    diagonal = row // 8 == column // 8
    slot = jnp.logical_and(diagonal, low3(column) == low3(row + 1))
    keep = jnp.logical_or(row // 8 < column // 8, jnp.logical_and(diagonal, jnp.logical_not(slot)))
    identity = (row == column).astype(F32)
    mirror = jnp.logical_and(diagonal, low3(row) == low3(column + 1))
    times = jnp.where(diagonal, jnp.where(slot, 0.0, jnp.where(mirror, 2.0, 1.0)), 2.0)
    groups = range(4)
    amats, drives, squares = [], [], []
    for g in groups:
        tiles = [in_ref[pl.ds((g % 2 * 4 + qq) * 2 + g // 2, 8, stride=24), :] for qq in range(4)]
        rows = []
        for kk in range(4):
            acc = jnp.zeros((8, LANES), F32)
            for qq in range(4):
                tile = tiles[qq]
                shift = (qq * K + kk * 8 - START[kk]) % LANES
                if shift:
                    tile = pltpu.roll(tile, shift, 1)
                inside = jnp.logical_and(lane >= qq * K + kk * 8, lane < qq * K + K)
                acc = jnp.where(inside, tile, acc)
            rows.append(acc)
        packed = jnp.concatenate(rows, axis=0)
        flipped = mirrored(packed, identity.astype(BF16), ones)
        amats.append(jnp.where(keep, packed, flipped) + (K - 1.0) * identity)
        square = packed + (K - 1.0) * identity
        square = jnp.sum(square * square * times, axis=0, keepdims=True)
        squares.append(jnp.broadcast_to(square, (8, LANES)))
        drive = jnp.sum(jnp.where(slot, packed, 0.0), axis=0, keepdims=True)
        drive = jnp.broadcast_to(drive, (8, LANES))
        drive = jnp.where(low3(lane) == 7, pltpu.roll(drive, 7, 1), pltpu.roll(drive, LANES - 1, 1))
        drives.append(drive[:1])
    sums = segment_sum(jnp.concatenate(squares, axis=0), ones)
    frobenius = [jnp.sqrt(sums[8 * g : 8 * g + 1]) for g in groups]
    root = [amats[g] / frobenius[g] for g in groups]
    inverse = [1.5 * identity - 0.5 * root[g] for g in groups]
    for step in range(NS - 1):
        blocks = [spread(root[g], ones) for g in groups]
        if step == 0:
            square = [product(thirds(root[g]), blocks[g], dot, 0) for g in groups]
        else:
            square = [product(thirds(root[g]), blocks[g], dot, 0) for g in groups]
            inverse = [1.5 * inverse[g] - 0.5 * product(thirds(inverse[g]), blocks[g], dot, 0) for g in groups]
        middle = [2.25 * identity - 1.5 * root[g] + 0.25 * square[g] for g in groups]
        root = [product(thirds(middle[g]), blocks[g], dot, 0) for g in groups]
    blocks = [spread(root[g], ones) for g in groups]
    inverse = [1.5 * inverse[g] - 0.5 * product(thirds(inverse[g]), blocks[g], dot, 0) for g in groups]
    for s0 in range(2):
        both = slice(2 * s0, 2 * s0 + 2)
        wide = jnp.concatenate(inverse[both], axis=1)
        state = jnp.concatenate(
            [in_ref[pl.ds(16 + s0 * 4 + kk, 8, stride=24), :] for kk in range(4)], axis=0
        )
        moved = product(thirds(wide), spread(state, point), dot, 0)
        first = segment_sum(wide * jnp.concatenate(drives[both], axis=1), point)
        norm = jnp.sqrt(segment_sum(jnp.concatenate(squares[both], axis=1), point)[:1])
        shift = jnp.sum(first * moved, axis=0, keepdims=True) / norm
        update = moved * (jnp.sqrt(K - 1.0) / jnp.sqrt(norm)) + shift
        for kk in range(4):
            out_ref[pl.ds(s0 * 4 + kk, 8, stride=8), :] = update[kk * 8 : kk * 8 + 8]


def swap(array, axis):
    return lax.all_to_all(array, axis, split_axis=0, concat_axis=0, tiled=True)


def local(state_ens, obs_ens, obs_value, obs_rinv, loc_weight, pair_block, pair_count):
    slab = lax.axis_index("grid").astype(jnp.int32).reshape(1)
    member = lax.axis_index("member").astype(jnp.int32).reshape(1)
    gathered = swap(obs_ens.reshape(OB * 4, LANES), "member")
    (mix,) = call(
        mix_kernel,
        (jax.ShapeDtypeStruct((LANES, 9 * OB), BF16),),
        slab,
        jnp.transpose(loc_weight, (1, 2, 0)),
        jnp.transpose(pair_block, (1, 0)),
        pair_count.reshape(1, SB),
        scalars=1,
        scratch=[pltpu.VMEM((3 * OB, LANES), F32)],
    )
    (terms,) = call(
        terms_kernel, (OB,), member, gathered, obs_value, obs_rinv, mix, scalars=1, unplaced=1
    )
    shares = swap(terms, "member")
    (windows,) = call(window_kernel, (4 * GRID,), shares)
    arrived = swap(windows.reshape(GRID, 4, LANES), "grid").reshape(4 * GRID, LANES)
    (combos,) = call(
        combine_kernel,
        (8 * 24,),
        arrived,
        mix,
        state_ens.reshape(SB * 4, LANES),
        scratch=[pltpu.VMEM((LANES, LANES), F32)],
    )
    matrices = swap(combos, "member")
    (update,) = call(transform_kernel, (SB * 4,), matrices)
    return swap(update.reshape(SB, 4, BV), "member")


def solution(mesh):
    return jax.shard_map(
        local,
        mesh=mesh,
        in_specs=(
            P("grid", "member", None),
            P("grid", "member", None),
            P("grid", None),
            P("grid", None),
            P("grid", None, None),
            P("grid", None),
            P("grid"),
        ),
        out_specs=P("grid", "member", None),
        check_vma=False,
    )
```

```python
import functools

import jax
import jax.numpy as jnp
from jax import lax
from jax.experimental import pallas as pl
from jax.experimental.pallas import tpu as pltpu
from jax.sharding import PartitionSpec as P

K = 32
BV = 128
Q = 8
P_SIZE = 8
NS = 7
SB = 16
OB = 128
MEMBERS = 8
GRID = 64
LANES = 128
F32 = jnp.float32
BF16 = jnp.bfloat16
HIGHEST = lax.Precision.HIGHEST
INTERPRET = False
VMEM_BYTES = 8 << 20

START = (0, 32, 56, 72)


def iota(shape, dim):
    return lax.broadcasted_iota(jnp.int32, shape, dim)


def low3(value):
    return jnp.bitwise_and(value, 7)


def thirds(value):
    high = value.astype(BF16)
    rest = value - high.astype(F32)
    middle = rest.astype(BF16)
    return high, middle, (rest - middle.astype(F32)).astype(BF16)


def dot(left, right):
    return jnp.dot(left, right, preferred_element_type=F32)


def dot_rows(left, right):
    return lax.dot_general(left, right, (((1,), (1,)), ((), ())), preferred_element_type=F32)


def product(left, right, form=dot, axis=0):
    high, middle, low = left
    first, second, third = right
    both = jnp.concatenate([high, middle], axis=1)
    return (
        form(both, jnp.concatenate([first] * 2, axis=axis))
        + form(both, jnp.concatenate([second] * 2, axis=axis))
        + form(jnp.concatenate([low, high], axis=1), jnp.concatenate([first, third], axis=axis))
    )


def call(kernel, outs, *args, scalars=0, unplaced=0, scratch=()):
    vmem = pl.BlockSpec(memory_space=pltpu.VMEM)
    return pl.pallas_call(
        kernel,
        out_shape=[
            out if isinstance(out, jax.ShapeDtypeStruct) else jax.ShapeDtypeStruct((out, LANES), F32)
            for out in outs
        ],
        in_specs=[pl.BlockSpec(memory_space=pltpu.SMEM)] * scalars
        + [vmem] * (len(args) - scalars - unplaced)
        + [pl.BlockSpec(memory_space=pl.ANY)] * unplaced,
        out_specs=[vmem] * len(outs),
        scratch_shapes=scratch,
        compiler_params=pltpu.CompilerParams(vmem_limit_bytes=VMEM_BYTES),
        interpret=INTERPRET,
        name=kernel.__name__,
    )(*args)


def mix_kernel(slab_ref, weight_ref, block_ref, count_ref, out_ref, mix_ref):
    picked = jnp.concatenate([block_ref[...]] * Q, axis=1)
    weight = jnp.concatenate([weight_ref[q] for q in range(Q)], axis=1)
    count = jnp.concatenate([count_ref[...]] * Q, axis=1)
    target = slab_ref[0] * OB + picked - OB
    used = jnp.logical_and(target >= 0, target < GRID * OB)
    used = jnp.logical_and(used, iota((P_SIZE, LANES), 0) < count)
    weight = jnp.where(used, weight, 0.0)
    step = 16
    block = iota((step, LANES), 0)
    for first in range(0, 3 * OB, step):
        mix = jnp.zeros((step, LANES), F32)
        for p in range(P_SIZE):
            mix = mix + jnp.where(block + first == picked[p : p + 1], weight[p : p + 1], 0.0)
        mix_ref[first : first + step] = mix
    out_ref[...] = jnp.concatenate(thirds(jnp.transpose(mix_ref[...])), axis=1)


def terms_kernel(member_ref, ens_ref, value_ref, rinv_ref, _, out_ref):
    start = pl.multiple_of(member_ref[0] * 16, 16)
    values = value_ref[pl.ds(start, 16), :]
    weights = rinv_ref[pl.ds(start, 16), :]
    lane = iota((8, LANES), 1)
    share = iota((8, LANES), 0)
    for four in range(4):
        perturbs, weighteds, vectors = [], [], []
        for row in range(four * 4, four * 4 + 4):
            tiles = [ens_ref[pl.ds(row * 4 + kk, 8, stride=64), :] for kk in range(4)]
            ensemble = jnp.concatenate(tiles, axis=0)
            mean = jnp.sum(ensemble, axis=0, keepdims=True) * (1.0 / K)
            perturb = ensemble - mean
            weighted = perturb * weights[row : row + 1, :]
            innovation = values[row : row + 1, :] - mean
            vectors.append(jnp.sum(weighted * innovation, axis=1, keepdims=True))
            perturbs.append(perturb)
            weighteds.append(weighted)
        grams = product(
            thirds(jnp.concatenate(weighteds, axis=0)),
            thirds(jnp.concatenate(perturbs, axis=0)),
            dot_rows,
            1,
        )
        terms = []
        for j in range(4):
            acc = None
            for kk in range(4):
                tile = grams[j * K + kk * 8 : j * K + kk * 8 + 8]
                shift = (START[kk] - kk * 8 - j * K) % LANES
                if shift:
                    tile = pltpu.roll(tile, shift, 1)
                slot = lane == START[kk] + low3(share + 1)
                tile = jnp.where(slot, vectors[j][kk * 8 : kk * 8 + 8], tile)
                acc = tile if acc is None else jnp.where(lane >= START[kk], tile, acc)
            terms.append(acc)
        for j in range(2):
            even = terms[2 * j]
            odd = pltpu.roll(terms[2 * j + 1], 64, 1)
            main = jnp.where(lane < 64, even, odd)
            rest = jnp.where(lane < 16, pltpu.roll(even, 64, 1), pltpu.roll(odd, 16, 1))
            out_ref[pl.ds(four * 2 + j, 8, stride=16), :] = main
            out_ref[pl.ds(8 + four * 2 + j, 8, stride=16), :] = rest


def window_kernel(in_ref, out_ref):
    main = jnp.concatenate([in_ref[m * 16 : m * 16 + 8] for m in range(8)], axis=0)
    rest = jnp.concatenate([in_ref[m * 16 + 8 : m * 16 + 16] for m in range(8)], axis=0)
    lane = iota((GRID, LANES), 1)
    out_ref[pl.ds(0, GRID, stride=4), :] = pltpu.roll(main, 1, 0)
    out_ref[pl.ds(1, GRID, stride=4), :] = main
    out_ref[pl.ds(2, GRID, stride=4), :] = pltpu.roll(main, GRID - 1, 0)
    before = pltpu.roll(rest, 1, 0)
    after = pltpu.roll(pltpu.roll(rest, GRID - 1, 0), 64, 1)
    here = pltpu.roll(rest, 32, 1)
    out_ref[pl.ds(3, GRID, stride=4), :] = jnp.where(
        lane < 32, before, jnp.where(lane < 64, here, after)
    )


def combine_kernel(in_ref, mix_ref, state_ref, out_ref, combo_ref):
    lane = iota((GRID, LANES), 1)
    rest = in_ref[pl.ds(3, GRID, stride=4), :]
    rows = []
    for d in range(3):
        main = in_ref[pl.ds(d, GRID, stride=4), :]
        for jb in range(2):
            first = pltpu.roll(main, 64, 1) if jb else main
            shift = (64 - d * 32 - jb * 16) % LANES
            last = pltpu.roll(rest, shift, 1) if shift else rest
            rows.append(jnp.where(lane < 64, first, last))
    high, middle, low = thirds(jnp.concatenate(rows, axis=0))
    mix = mix_ref[...]
    combo_ref[...] = (
        dot(mix, jnp.concatenate([high] * 3, axis=0))
        + dot(mix[:, : 6 * OB], jnp.concatenate([middle] * 2, axis=0))
        + dot(mix[:, : 3 * OB], low)
    )
    for q in range(Q):
        for s0 in range(2):
            out_ref[pl.ds(q * 2 + s0, 8, stride=24), :] = combo_ref[pl.ds(q * 16 + s0, 8, stride=2), :]
    for r in range(8):
        out_ref[pl.ds(16 + r, 8, stride=24), :] = state_ref[pl.ds(r, 8, stride=8), :]


def spread(value, mask):
    blocks = mask.shape[0] // value.shape[0]
    return [jnp.concatenate([third] * blocks, axis=0) * mask for third in thirds(value)]


def segment_sum(value, ones):
    rows = value.shape[0]
    wide = dot(jnp.concatenate(thirds(value), axis=0), ones)
    return wide[:rows] + wide[rows : 2 * rows] + wide[2 * rows :]


def mirrored(value, identity, ones):
    high, middle, low = [jnp.concatenate([third] * 4, axis=0) * ones for third in thirds(value)]
    return dot_rows(
        jnp.concatenate([identity] * 2, axis=1), jnp.concatenate([high, middle], axis=1)
    ) + dot_rows(identity, low)


def transform_kernel(in_ref, out_ref):
    def same(shape, rows, lanes):
        return (iota(shape, 0) // rows == iota(shape, 1) // lanes).astype(F32).astype(BF16)

    ones = same((LANES, LANES), K, K)
    point = same((Q * K, BV), K, BV // Q)
    lane = iota((8, LANES), 1)
    row = iota((K, LANES), 0)
    column = jnp.bitwise_and(iota((K, LANES), 1), K - 1)
    diagonal = row // 8 == column // 8
    slot = jnp.logical_and(diagonal, low3(column) == low3(row + 1))
    keep = jnp.logical_or(row // 8 < column // 8, jnp.logical_and(diagonal, jnp.logical_not(slot)))
    identity = (row == column).astype(F32)
    mirror = jnp.logical_and(diagonal, low3(row) == low3(column + 1))
    times = jnp.where(diagonal, jnp.where(slot, 0.0, jnp.where(mirror, 2.0, 1.0)), 2.0)
    groups = range(4)
    amats, drives, squares = [], [], []
    for g in groups:
        tiles = [in_ref[pl.ds((g % 2 * 4 + qq) * 2 + g // 2, 8, stride=24), :] for qq in range(4)]
        rows = []
        for kk in range(4):
            acc = jnp.zeros((8, LANES), F32)
            for qq in range(4):
                tile = tiles[qq]
                shift = (qq * K + kk * 8 - START[kk]) % LANES
                if shift:
                    tile = pltpu.roll(tile, shift, 1)
                inside = jnp.logical_and(lane >= qq * K + kk * 8, lane < qq * K + K)
                acc = jnp.where(inside, tile, acc)
            rows.append(acc)
        packed = jnp.concatenate(rows, axis=0)
        flipped = mirrored(packed, identity.astype(BF16), ones)
        amats.append(jnp.where(keep, packed, flipped) + (K - 1.0) * identity)
        square = packed + (K - 1.0) * identity
        square = jnp.sum(square * square * times, axis=0, keepdims=True)
        squares.append(jnp.broadcast_to(square, (8, LANES)))
        drive = jnp.sum(jnp.where(slot, packed, 0.0), axis=0, keepdims=True)
        drive = jnp.broadcast_to(drive, (8, LANES))
        drive = jnp.where(low3(lane) == 7, pltpu.roll(drive, 7, 1), pltpu.roll(drive, LANES - 1, 1))
        drives.append(drive[:1])
    sums = segment_sum(jnp.concatenate(squares, axis=0), ones)
    frobenius = [jnp.sqrt(sums[8 * g : 8 * g + 1]) for g in groups]
    root = [amats[g] / frobenius[g] for g in groups]
    inverse = [1.5 * identity - 0.5 * root[g] for g in groups]
    for step in range(NS - 1):
        blocks = [spread(root[g], ones) for g in groups]
        if step == 0:
            square = [product(thirds(root[g]), blocks[g]) for g in groups]
        else:
            square = [product(thirds(root[g]), blocks[g]) for g in groups]
        middle = [2.25 * identity - 1.5 * root[g] + 0.25 * square[g] for g in groups]
        if step == 0:
            root = [product(thirds(middle[g]), blocks[g]) for g in groups]
        else:
            both = [
                product(thirds(jnp.concatenate([middle[g], inverse[g]], axis=0)), blocks[g])
                for g in groups
            ]
            root = [both[g][:K] for g in groups]
            inverse = [1.5 * inverse[g] - 0.5 * both[g][K:] for g in groups]
    blocks = [spread(root[g], ones) for g in groups]
    inverse = [1.5 * inverse[g] - 0.5 * product(thirds(inverse[g]), blocks[g]) for g in groups]
    for s0 in range(2):
        both = slice(2 * s0, 2 * s0 + 2)
        wide = jnp.concatenate(inverse[both], axis=1)
        state = jnp.concatenate(
            [in_ref[pl.ds(16 + s0 * 4 + kk, 8, stride=24), :] for kk in range(4)], axis=0
        )
        moved = product(thirds(wide), spread(state, point))
        first = segment_sum(wide * jnp.concatenate(drives[both], axis=1), point)
        norm = jnp.sqrt(segment_sum(jnp.concatenate(squares[both], axis=1), point)[:1])
        shift = jnp.sum(first * moved, axis=0, keepdims=True) / norm
        update = moved * (jnp.sqrt(K - 1.0) / jnp.sqrt(norm)) + shift
        for kk in range(4):
            out_ref[pl.ds(s0 * 4 + kk, 8, stride=8), :] = update[kk * 8 : kk * 8 + 8]


def swap(array, axis):
    return lax.all_to_all(array, axis, split_axis=0, concat_axis=0, tiled=True)


def local(state_ens, obs_ens, obs_value, obs_rinv, loc_weight, pair_block, pair_count):
    slab = lax.axis_index("grid").astype(jnp.int32).reshape(1)
    member = lax.axis_index("member").astype(jnp.int32).reshape(1)
    gathered = swap(obs_ens.reshape(OB * 4, LANES), "member")
    (mix,) = call(
        mix_kernel,
        (jax.ShapeDtypeStruct((LANES, 9 * OB), BF16),),
        slab,
        jnp.transpose(loc_weight, (1, 2, 0)),
        jnp.transpose(pair_block, (1, 0)),
        pair_count.reshape(1, SB),
        scalars=1,
        scratch=[pltpu.VMEM((3 * OB, LANES), F32)],
    )
    (terms,) = call(
        terms_kernel, (OB,), member, gathered, obs_value, obs_rinv, mix, scalars=1, unplaced=1
    )
    shares = swap(terms, "member")
    (windows,) = call(window_kernel, (4 * GRID,), shares)
    arrived = swap(windows.reshape(GRID, 4, LANES), "grid").reshape(4 * GRID, LANES)
    (combos,) = call(
        combine_kernel,
        (8 * 24,),
        arrived,
        mix,
        state_ens.reshape(SB * 4, LANES),
        scratch=[pltpu.VMEM((LANES, LANES), F32)],
    )
    matrices = swap(combos, "member")
    (update,) = call(transform_kernel, (SB * 4,), matrices)
    return swap(update.reshape(SB, 4, BV), "member")


def solution(mesh):
    return jax.shard_map(
        local,
        mesh=mesh,
        in_specs=(
            P("grid", "member", None),
            P("grid", "member", None),
            P("grid", None),
            P("grid", None),
            P("grid", None, None),
            P("grid", None),
            P("grid"),
        ),
        out_specs=P("grid", "member", None),
        check_vma=False,
    )
```

```python
import functools

import jax
import jax.numpy as jnp
from jax import lax
from jax.experimental import pallas as pl
from jax.experimental.pallas import tpu as pltpu
from jax.sharding import PartitionSpec as P

K = 32
BV = 128
Q = 8
P_SIZE = 8
NS = 7
SB = 16
OB = 128
MEMBERS = 8
GRID = 64
LANES = 128
F32 = jnp.float32
BF16 = jnp.bfloat16
HIGHEST = lax.Precision.HIGHEST
INTERPRET = False
VMEM_BYTES = 8 << 20

START = (0, 32, 56, 72)


def iota(shape, dim):
    return lax.broadcasted_iota(jnp.int32, shape, dim)


def low3(value):
    return jnp.bitwise_and(value, 7)


def thirds(value):
    high = value.astype(BF16)
    rest = value - high.astype(F32)
    middle = rest.astype(BF16)
    return high, middle, (rest - middle.astype(F32)).astype(BF16)


def dot(left, right):
    return jnp.dot(left, right, preferred_element_type=F32)


def dot_rows(left, right):
    return lax.dot_general(left, right, (((1,), (1,)), ((), ())), preferred_element_type=F32)


def product(left, right, form=dot, axis=0):
    high, middle, low = left
    first, second, third = right
    if axis:
        return form(
            jnp.concatenate([high, low, middle, middle, high, high], axis=1),
            jnp.concatenate([third, first, second, first, second, first], axis=1),
        )
    both = jnp.concatenate([high, middle], axis=1)
    return (
        form(both, jnp.concatenate([first] * 2, axis=axis))
        + form(both, jnp.concatenate([second] * 2, axis=axis))
        + form(jnp.concatenate([low, high], axis=1), jnp.concatenate([first, third], axis=axis))
    )


def call(kernel, outs, *args, scalars=0, unplaced=0, scratch=()):
    vmem = pl.BlockSpec(memory_space=pltpu.VMEM)
    return pl.pallas_call(
        kernel,
        out_shape=[
            out if isinstance(out, jax.ShapeDtypeStruct) else jax.ShapeDtypeStruct((out, LANES), F32)
            for out in outs
        ],
        in_specs=[pl.BlockSpec(memory_space=pltpu.SMEM)] * scalars
        + [vmem] * (len(args) - scalars - unplaced)
        + [pl.BlockSpec(memory_space=pl.ANY)] * unplaced,
        out_specs=[vmem] * len(outs),
        scratch_shapes=scratch,
        compiler_params=pltpu.CompilerParams(vmem_limit_bytes=VMEM_BYTES),
        interpret=INTERPRET,
        name=kernel.__name__,
    )(*args)


def mix_kernel(slab_ref, weight_ref, block_ref, count_ref, out_ref, mix_ref):
    picked = jnp.concatenate([block_ref[...]] * Q, axis=1)
    weight = jnp.concatenate([weight_ref[q] for q in range(Q)], axis=1)
    count = jnp.concatenate([count_ref[...]] * Q, axis=1)
    target = slab_ref[0] * OB + picked - OB
    used = jnp.logical_and(target >= 0, target < GRID * OB)
    used = jnp.logical_and(used, iota((P_SIZE, LANES), 0) < count)
    weight = jnp.where(used, weight, 0.0)
    step = 16
    block = iota((step, LANES), 0)
    for first in range(0, 3 * OB, step):
        mix = jnp.zeros((step, LANES), F32)
        for p in range(P_SIZE):
            mix = mix + jnp.where(block + first == picked[p : p + 1], weight[p : p + 1], 0.0)
        mix_ref[first : first + step] = mix
    out_ref[...] = jnp.concatenate(thirds(jnp.transpose(mix_ref[...])), axis=1)


def terms_kernel(member_ref, ens_ref, value_ref, rinv_ref, _, out_ref):
    start = pl.multiple_of(member_ref[0] * 16, 16)
    values = value_ref[pl.ds(start, 16), :]
    weights = rinv_ref[pl.ds(start, 16), :]
    lane = iota((8, LANES), 1)
    share = iota((8, LANES), 0)
    for four in range(4):
        perturbs, weighteds, vectors = [], [], []
        for row in range(four * 4, four * 4 + 4):
            tiles = [ens_ref[pl.ds(row * 4 + kk, 8, stride=64), :] for kk in range(4)]
            ensemble = jnp.concatenate(tiles, axis=0)
            mean = jnp.sum(ensemble, axis=0, keepdims=True) * (1.0 / K)
            perturb = ensemble - mean
            weighted = perturb * weights[row : row + 1, :]
            innovation = values[row : row + 1, :] - mean
            vectors.append(jnp.sum(weighted * innovation, axis=1, keepdims=True))
            perturbs.append(perturb)
            weighteds.append(weighted)
        grams = product(
            thirds(jnp.concatenate(weighteds, axis=0)),
            thirds(jnp.concatenate(perturbs, axis=0)),
            dot_rows,
            1,
        )
        terms = []
        for j in range(4):
            acc = None
            for kk in range(4):
                tile = grams[j * K + kk * 8 : j * K + kk * 8 + 8]
                shift = (START[kk] - kk * 8 - j * K) % LANES
                if shift:
                    tile = pltpu.roll(tile, shift, 1)
                slot = lane == START[kk] + low3(share + 1)
                tile = jnp.where(slot, vectors[j][kk * 8 : kk * 8 + 8], tile)
                acc = tile if acc is None else jnp.where(lane >= START[kk], tile, acc)
            terms.append(acc)
        for j in range(2):
            even = terms[2 * j]
            odd = pltpu.roll(terms[2 * j + 1], 64, 1)
            main = jnp.where(lane < 64, even, odd)
            rest = jnp.where(lane < 16, pltpu.roll(even, 64, 1), pltpu.roll(odd, 16, 1))
            out_ref[pl.ds(four * 2 + j, 8, stride=16), :] = main
            out_ref[pl.ds(8 + four * 2 + j, 8, stride=16), :] = rest


def window_kernel(in_ref, out_ref):
    main = jnp.concatenate([in_ref[m * 16 : m * 16 + 8] for m in range(8)], axis=0)
    rest = jnp.concatenate([in_ref[m * 16 + 8 : m * 16 + 16] for m in range(8)], axis=0)
    lane = iota((GRID, LANES), 1)
    out_ref[pl.ds(0, GRID, stride=4), :] = pltpu.roll(main, 1, 0)
    out_ref[pl.ds(1, GRID, stride=4), :] = main
    out_ref[pl.ds(2, GRID, stride=4), :] = pltpu.roll(main, GRID - 1, 0)
    before = pltpu.roll(rest, 1, 0)
    after = pltpu.roll(pltpu.roll(rest, GRID - 1, 0), 64, 1)
    here = pltpu.roll(rest, 32, 1)
    out_ref[pl.ds(3, GRID, stride=4), :] = jnp.where(
        lane < 32, before, jnp.where(lane < 64, here, after)
    )


def combine_kernel(in_ref, mix_ref, state_ref, out_ref, combo_ref):
    lane = iota((GRID, LANES), 1)
    rest = in_ref[pl.ds(3, GRID, stride=4), :]
    rows = []
    for d in range(3):
        main = in_ref[pl.ds(d, GRID, stride=4), :]
        for jb in range(2):
            first = pltpu.roll(main, 64, 1) if jb else main
            shift = (64 - d * 32 - jb * 16) % LANES
            last = pltpu.roll(rest, shift, 1) if shift else rest
            rows.append(jnp.where(lane < 64, first, last))
    high, middle, low = thirds(jnp.concatenate(rows, axis=0))
    mix = mix_ref[...]
    combo_ref[...] = (
        dot(mix, jnp.concatenate([high] * 3, axis=0))
        + dot(mix[:, : 6 * OB], jnp.concatenate([middle] * 2, axis=0))
        + dot(mix[:, : 3 * OB], low)
    )
    for q in range(Q):
        for s0 in range(2):
            out_ref[pl.ds(q * 2 + s0, 8, stride=24), :] = combo_ref[pl.ds(q * 16 + s0, 8, stride=2), :]
    for r in range(8):
        out_ref[pl.ds(16 + r, 8, stride=24), :] = state_ref[pl.ds(r, 8, stride=8), :]


def spread(value, mask):
    blocks = mask.shape[0] // value.shape[0]
    return [jnp.concatenate([third] * blocks, axis=0) * mask for third in thirds(value)]


def segment_sum(value, ones):
    rows = value.shape[0]
    wide = dot(jnp.concatenate(thirds(value), axis=0), ones)
    return wide[:rows] + wide[rows : 2 * rows] + wide[2 * rows :]


def transform_kernel(in_ref, out_ref):
    def same(shape, rows, lanes):
        return (iota(shape, 0) // rows == iota(shape, 1) // lanes).astype(F32).astype(BF16)

    ones = same((LANES, LANES), K, K)
    point = same((Q * K, BV), K, BV // Q)
    lane = iota((8, LANES), 1)
    row = iota((K, LANES), 0)
    column = jnp.bitwise_and(iota((K, LANES), 1), K - 1)
    diagonal = row // 8 == column // 8
    slot = jnp.logical_and(diagonal, low3(column) == low3(row + 1))
    keep = jnp.logical_or(row // 8 < column // 8, jnp.logical_and(diagonal, jnp.logical_not(slot)))
    identity = (row == column).astype(F32)
    mirror = jnp.logical_and(diagonal, low3(row) == low3(column + 1))
    times = jnp.where(diagonal, jnp.where(slot, 0.0, jnp.where(mirror, 2.0, 1.0)), 2.0)
    groups = range(4)
    amats, drives, squares = [], [], []
    for g in groups:
        tiles = [in_ref[pl.ds((g % 2 * 4 + qq) * 2 + g // 2, 8, stride=24), :] for qq in range(4)]
        rows = []
        for kk in range(4):
            acc = jnp.zeros((8, LANES), F32)
            for qq in range(4):
                tile = tiles[qq]
                shift = (qq * K + kk * 8 - START[kk]) % LANES
                if shift:
                    tile = pltpu.roll(tile, shift, 1)
                inside = jnp.logical_and(lane >= qq * K + kk * 8, lane < qq * K + K)
                acc = jnp.where(inside, tile, acc)
            rows.append(acc)
        packed = jnp.concatenate(rows, axis=0)
        upright = jnp.transpose(packed)
        flipped = jnp.concatenate([upright[q * K : q * K + K] for q in range(4)], axis=1)
        amats.append(jnp.where(keep, packed, flipped) + (K - 1.0) * identity)
        square = packed + (K - 1.0) * identity
        square = jnp.sum(square * square * times, axis=0, keepdims=True)
        squares.append(jnp.broadcast_to(square, (8, LANES)))
        drive = jnp.sum(jnp.where(slot, packed, 0.0), axis=0, keepdims=True)
        drive = jnp.broadcast_to(drive, (8, LANES))
        drive = jnp.where(low3(lane) == 7, pltpu.roll(drive, 7, 1), pltpu.roll(drive, LANES - 1, 1))
        drives.append(drive[:1])
    sums = segment_sum(jnp.concatenate(squares, axis=0), ones)
    frobenius = [jnp.sqrt(sums[8 * g : 8 * g + 1]) for g in groups]
    root = [amats[g] / frobenius[g] for g in groups]
    inverse = [1.5 * identity - 0.5 * root[g] for g in groups]
    blocks = [spread(amats[g], ones) for g in groups]
    for step in range(NS - 1):
        if step == 0:
            square = [product(thirds(amats[g]), blocks[g]) / sums[8 * g : 8 * g + 1] for g in groups]
        else:
            blocks = [spread(root[g], ones) for g in groups]
            square = [product(thirds(root[g]), blocks[g]) for g in groups]
        middle = [2.25 * identity - 1.5 * root[g] + 0.25 * square[g] for g in groups]
        if step == 0:
            root = [product(thirds(middle[g]), blocks[g]) / frobenius[g] for g in groups]
        else:
            both = [
                product(thirds(jnp.concatenate([middle[g], inverse[g]], axis=0)), blocks[g])
                for g in groups
            ]
            root = [both[g][:K] for g in groups]
            inverse = [1.5 * inverse[g] - 0.5 * both[g][K:] for g in groups]
    blocks = [spread(root[g], ones) for g in groups]
    inverse = [1.5 * inverse[g] - 0.5 * product(thirds(inverse[g]), blocks[g]) for g in groups]
    for s0 in range(2):
        both = slice(2 * s0, 2 * s0 + 2)
        wide = jnp.concatenate(inverse[both], axis=1)
        state = jnp.concatenate(
            [in_ref[pl.ds(16 + s0 * 4 + kk, 8, stride=24), :] for kk in range(4)], axis=0
        )
        moved = product(thirds(wide), spread(state, point))
        first = segment_sum(wide * jnp.concatenate(drives[both], axis=1), point)
        norm = jnp.sqrt(segment_sum(jnp.concatenate(squares[both], axis=1), point)[:1])
        shift = jnp.sum(first * moved, axis=0, keepdims=True) / norm
        update = moved * (jnp.sqrt(K - 1.0) / jnp.sqrt(norm)) + shift
        for kk in range(4):
            out_ref[pl.ds(s0 * 4 + kk, 8, stride=8), :] = update[kk * 8 : kk * 8 + 8]


def swap(array, axis):
    return lax.all_to_all(array, axis, split_axis=0, concat_axis=0, tiled=True)


def local(state_ens, obs_ens, obs_value, obs_rinv, loc_weight, pair_block, pair_count):
    slab = lax.axis_index("grid").astype(jnp.int32).reshape(1)
    member = lax.axis_index("member").astype(jnp.int32).reshape(1)
    gathered = swap(obs_ens.reshape(OB * 4, LANES), "member")
    (mix,) = call(
        mix_kernel,
        (jax.ShapeDtypeStruct((LANES, 9 * OB), BF16),),
        slab,
        jnp.transpose(loc_weight, (1, 2, 0)),
        jnp.transpose(pair_block, (1, 0)),
        pair_count.reshape(1, SB),
        scalars=1,
        scratch=[pltpu.VMEM((3 * OB, LANES), F32)],
    )
    (terms,) = call(
        terms_kernel, (OB,), member, gathered, obs_value, obs_rinv, mix, scalars=1, unplaced=1
    )
    shares = swap(terms, "member")
    (windows,) = call(window_kernel, (4 * GRID,), shares)
    arrived = swap(windows.reshape(GRID, 4, LANES), "grid").reshape(4 * GRID, LANES)
    (combos,) = call(
        combine_kernel,
        (8 * 24,),
        arrived,
        mix,
        state_ens.reshape(SB * 4, LANES),
        scratch=[pltpu.VMEM((LANES, LANES), F32)],
    )
    matrices = swap(combos, "member")
    (update,) = call(transform_kernel, (SB * 4,), matrices)
    return swap(update.reshape(SB, 4, BV), "member")


def solution(mesh):
    return jax.shard_map(
        local,
        mesh=mesh,
        in_specs=(
            P("grid", "member", None),
            P("grid", "member", None),
            P("grid", None),
            P("grid", None),
            P("grid", None, None),
            P("grid", None),
            P("grid"),
        ),
        out_specs=P("grid", "member", None),
        check_vma=False,
    )
```

```python
import functools

import jax
import jax.numpy as jnp
from jax import lax
from jax.experimental import pallas as pl
from jax.experimental.pallas import tpu as pltpu
from jax.sharding import PartitionSpec as P

K = 32
BV = 128
Q = 8
P_SIZE = 8
NS = 7
SB = 16
OB = 128
MEMBERS = 8
GRID = 64
LANES = 128
F32 = jnp.float32
BF16 = jnp.bfloat16
HIGHEST = lax.Precision.HIGHEST
INTERPRET = False
VMEM_BYTES = 8 << 20

START = (0, 32, 56, 72)


def iota(shape, dim):
    return lax.broadcasted_iota(jnp.int32, shape, dim)


def low3(value):
    return jnp.bitwise_and(value, 7)


def thirds(value):
    high = value.astype(BF16)
    rest = value - high.astype(F32)
    middle = rest.astype(BF16)
    return high, middle, (rest - middle.astype(F32)).astype(BF16)


def dot(left, right):
    return jnp.dot(left, right, preferred_element_type=F32)


def dot_rows(left, right):
    return lax.dot_general(left, right, (((1,), (1,)), ((), ())), preferred_element_type=F32)


def product(left, right, form=dot, axis=0):
    high, middle, low = left
    first, second, third = right
    both = jnp.concatenate([high, middle], axis=1)
    return (
        form(both, jnp.concatenate([first] * 2, axis=axis))
        + form(both, jnp.concatenate([second] * 2, axis=axis))
        + form(jnp.concatenate([low, high], axis=1), jnp.concatenate([first, third], axis=axis))
    )


def call(kernel, outs, *args, scalars=0, unplaced=0, scratch=()):
    vmem = pl.BlockSpec(memory_space=pltpu.VMEM)
    return pl.pallas_call(
        kernel,
        out_shape=[
            out if isinstance(out, jax.ShapeDtypeStruct) else jax.ShapeDtypeStruct((out, LANES), F32)
            for out in outs
        ],
        in_specs=[pl.BlockSpec(memory_space=pltpu.SMEM)] * scalars
        + [vmem] * (len(args) - scalars - unplaced)
        + [pl.BlockSpec(memory_space=pl.ANY)] * unplaced,
        out_specs=[vmem] * len(outs),
        scratch_shapes=scratch,
        compiler_params=pltpu.CompilerParams(vmem_limit_bytes=VMEM_BYTES),
        interpret=INTERPRET,
        name=kernel.__name__,
    )(*args)


def mix_kernel(slab_ref, weight_ref, block_ref, count_ref, out_ref, mix_ref):
    picked = jnp.concatenate([block_ref[...]] * Q, axis=1)
    weight = jnp.concatenate([weight_ref[q] for q in range(Q)], axis=1)
    count = jnp.concatenate([count_ref[...]] * Q, axis=1)
    target = slab_ref[0] * OB + picked - OB
    used = jnp.logical_and(target >= 0, target < GRID * OB)
    used = jnp.logical_and(used, iota((P_SIZE, LANES), 0) < count)
    weight = jnp.where(used, weight, 0.0)
    step = 16
    block = iota((step, LANES), 0)
    for first in range(0, 3 * OB, step):
        mix = jnp.zeros((step, LANES), F32)
        for p in range(P_SIZE):
            mix = mix + jnp.where(block + first == picked[p : p + 1], weight[p : p + 1], 0.0)
        mix_ref[first : first + step] = mix
    out_ref[...] = jnp.concatenate(thirds(jnp.transpose(mix_ref[...])), axis=1)


def terms_kernel(member_ref, ens_ref, value_ref, rinv_ref, _, out_ref):
    start = pl.multiple_of(member_ref[0] * 16, 16)
    values = value_ref[pl.ds(start, 16), :]
    weights = rinv_ref[pl.ds(start, 16), :]
    lane = iota((8, LANES), 1)
    share = iota((8, LANES), 0)
    for four in range(4):
        perturbs, weighteds, vectors = [], [], []
        for row in range(four * 4, four * 4 + 4):
            tiles = [ens_ref[pl.ds(row * 4 + kk, 8, stride=64), :] for kk in range(4)]
            ensemble = jnp.concatenate(tiles, axis=0)
            mean = jnp.sum(ensemble, axis=0, keepdims=True) * (1.0 / K)
            perturb = ensemble - mean
            weighted = perturb * weights[row : row + 1, :]
            innovation = values[row : row + 1, :] - mean
            vectors.append(jnp.sum(weighted * innovation, axis=1, keepdims=True))
            perturbs.append(perturb)
            weighteds.append(weighted)
        grams = product(
            thirds(jnp.concatenate(weighteds, axis=0)),
            thirds(jnp.concatenate(perturbs, axis=0)),
            dot_rows,
            1,
        )
        terms = []
        for j in range(4):
            acc = None
            for kk in range(4):
                tile = grams[j * K + kk * 8 : j * K + kk * 8 + 8]
                shift = (START[kk] - kk * 8 - j * K) % LANES
                if shift:
                    tile = pltpu.roll(tile, shift, 1)
                slot = lane == START[kk] + low3(share + 1)
                tile = jnp.where(slot, vectors[j][kk * 8 : kk * 8 + 8], tile)
                acc = tile if acc is None else jnp.where(lane >= START[kk], tile, acc)
            terms.append(acc)
        for j in range(2):
            even = terms[2 * j]
            odd = pltpu.roll(terms[2 * j + 1], 64, 1)
            main = jnp.where(lane < 64, even, odd)
            rest = jnp.where(lane < 16, pltpu.roll(even, 64, 1), pltpu.roll(odd, 16, 1))
            out_ref[pl.ds(four * 2 + j, 8, stride=16), :] = main
            out_ref[pl.ds(8 + four * 2 + j, 8, stride=16), :] = rest


def window_kernel(in_ref, out_ref):
    main = jnp.concatenate([in_ref[m * 16 : m * 16 + 8] for m in range(8)], axis=0)
    rest = jnp.concatenate([in_ref[m * 16 + 8 : m * 16 + 16] for m in range(8)], axis=0)
    lane = iota((GRID, LANES), 1)
    out_ref[pl.ds(0, GRID, stride=4), :] = pltpu.roll(main, 1, 0)
    out_ref[pl.ds(1, GRID, stride=4), :] = main
    out_ref[pl.ds(2, GRID, stride=4), :] = pltpu.roll(main, GRID - 1, 0)
    before = pltpu.roll(rest, 1, 0)
    after = pltpu.roll(pltpu.roll(rest, GRID - 1, 0), 64, 1)
    here = pltpu.roll(rest, 32, 1)
    out_ref[pl.ds(3, GRID, stride=4), :] = jnp.where(
        lane < 32, before, jnp.where(lane < 64, here, after)
    )


def combine_kernel(in_ref, mix_ref, state_ref, out_ref, combo_ref):
    lane = iota((GRID, LANES), 1)
    rest = in_ref[pl.ds(3, GRID, stride=4), :]
    rows = []
    for d in range(3):
        main = in_ref[pl.ds(d, GRID, stride=4), :]
        for jb in range(2):
            first = pltpu.roll(main, 64, 1) if jb else main
            shift = (64 - d * 32 - jb * 16) % LANES
            last = pltpu.roll(rest, shift, 1) if shift else rest
            rows.append(jnp.where(lane < 64, first, last))
    high, middle, low = thirds(jnp.concatenate(rows, axis=0))
    mix = mix_ref[...]
    combo_ref[...] = (
        dot(mix, jnp.concatenate([high] * 3, axis=0))
        + dot(mix[:, : 6 * OB], jnp.concatenate([middle] * 2, axis=0))
        + dot(mix[:, : 3 * OB], low)
    )
    for q in range(Q):
        for s0 in range(2):
            out_ref[pl.ds(q * 2 + s0, 8, stride=24), :] = combo_ref[pl.ds(q * 16 + s0, 8, stride=2), :]
    for r in range(8):
        out_ref[pl.ds(16 + r, 8, stride=24), :] = state_ref[pl.ds(r, 8, stride=8), :]


def spread(value, mask):
    blocks = mask.shape[0] // value.shape[0]
    return [jnp.concatenate([third] * blocks, axis=0) * mask for third in thirds(value)]


def segment_sum(value, ones):
    rows = value.shape[0]
    wide = dot(jnp.concatenate(thirds(value), axis=0), ones)
    return wide[:rows] + wide[rows : 2 * rows] + wide[2 * rows :]


def mirrored(value, identity, ones):
    high, middle, low = [jnp.concatenate([third] * 4, axis=0) * ones for third in thirds(value)]
    return dot_rows(
        jnp.concatenate([identity] * 2, axis=1), jnp.concatenate([high, middle], axis=1)
    ) + dot_rows(identity, low)


def transform_kernel(in_ref, out_ref):
    def same(shape, rows, lanes):
        return (iota(shape, 0) // rows == iota(shape, 1) // lanes).astype(F32).astype(BF16)

    ones = same((LANES, LANES), K, K)
    point = same((Q * K, BV), K, BV // Q)
    lane = iota((8, LANES), 1)
    row = iota((K, LANES), 0)
    column = jnp.bitwise_and(iota((K, LANES), 1), K - 1)
    diagonal = row // 8 == column // 8
    slot = jnp.logical_and(diagonal, low3(column) == low3(row + 1))
    keep = jnp.logical_or(row // 8 < column // 8, jnp.logical_and(diagonal, jnp.logical_not(slot)))
    identity = (row == column).astype(F32)
    mirror = jnp.logical_and(diagonal, low3(row) == low3(column + 1))
    times = jnp.where(diagonal, jnp.where(slot, 0.0, jnp.where(mirror, 2.0, 1.0)), 2.0)
    groups = range(4)
    amats, drives, squares = [], [], []
    for g in groups:
        tiles = [in_ref[pl.ds((g % 2 * 4 + qq) * 2 + g // 2, 8, stride=24), :] for qq in range(4)]
        rows = []
        for kk in range(4):
            acc = jnp.zeros((8, LANES), F32)
            for qq in range(4):
                tile = tiles[qq]
                shift = (qq * K + kk * 8 - START[kk]) % LANES
                if shift:
                    tile = pltpu.roll(tile, shift, 1)
                inside = jnp.logical_and(lane >= qq * K + kk * 8, lane < qq * K + K)
                acc = jnp.where(inside, tile, acc)
            rows.append(acc)
        packed = jnp.concatenate(rows, axis=0)
        flipped = mirrored(packed, identity.astype(BF16), ones)
        amats.append(jnp.where(keep, packed, flipped) + (K - 1.0) * identity)
        square = packed + (K - 1.0) * identity
        square = jnp.sum(square * square * times, axis=0, keepdims=True)
        squares.append(jnp.broadcast_to(square, (8, LANES)))
        drive = jnp.sum(jnp.where(slot, packed, 0.0), axis=0, keepdims=True)
        drive = jnp.broadcast_to(drive, (8, LANES))
        drive = jnp.where(low3(lane) == 7, pltpu.roll(drive, 7, 1), pltpu.roll(drive, LANES - 1, 1))
        drives.append(drive[:1])
    sums = segment_sum(jnp.concatenate(squares, axis=0), ones)
    frobenius = [jnp.sqrt(sums[8 * g : 8 * g + 1]) for g in groups]
    root = [amats[g] / frobenius[g] for g in groups]
    inverse = [1.5 * identity - 0.5 * root[g] for g in groups]
    for step in range(NS - 1):
        blocks = [spread(root[g], ones) for g in groups]
        if step == 0:
            square = [product(thirds(root[g]), blocks[g]) for g in groups]
        else:
            square = [product(thirds(root[g]), blocks[g]) for g in groups]
        middle = [2.25 * identity - 1.5 * root[g] + 0.25 * square[g] for g in groups]
        if step == 0:
            root = [product(thirds(middle[g]), blocks[g]) for g in groups]
        else:
            both = [
                product(thirds(jnp.concatenate([middle[g], inverse[g]], axis=0)), blocks[g])
                for g in groups
            ]
            root = [both[g][:K] for g in groups]
            inverse = [1.5 * inverse[g] - 0.5 * both[g][K:] for g in groups]
    blocks = [spread(root[g], ones) for g in groups]
    inverse = [1.5 * inverse[g] - 0.5 * product(thirds(inverse[g]), blocks[g]) for g in groups]
    for s0 in range(2):
        both = slice(2 * s0, 2 * s0 + 2)
        wide = jnp.concatenate(inverse[both], axis=1)
        state = jnp.concatenate(
            [in_ref[pl.ds(16 + s0 * 4 + kk, 8, stride=24), :] for kk in range(4)], axis=0
        )
        moved = product(thirds(wide), spread(state, point))
        first = segment_sum(wide * jnp.concatenate(drives[both], axis=1), point)
        norm = jnp.sqrt(segment_sum(jnp.concatenate(squares[both], axis=1), point)[:1])
        shift = jnp.sum(first * moved, axis=0, keepdims=True) / norm
        update = moved * (jnp.sqrt(K - 1.0) / jnp.sqrt(norm)) + shift
        for kk in range(4):
            out_ref[pl.ds(s0 * 4 + kk, 8, stride=8), :] = update[kk * 8 : kk * 8 + 8]


def swap(array, axis):
    return lax.all_to_all(array, axis, split_axis=0, concat_axis=0, tiled=True)


def local(state_ens, obs_ens, obs_value, obs_rinv, loc_weight, pair_block, pair_count):
    slab = lax.axis_index("grid").astype(jnp.int32).reshape(1)
    member = lax.axis_index("member").astype(jnp.int32).reshape(1)
    gathered = swap(obs_ens.reshape(OB * 4, LANES), "member")
    (mix,) = call(
        mix_kernel,
        (jax.ShapeDtypeStruct((LANES, 9 * OB), BF16),),
        slab,
        jnp.transpose(loc_weight, (1, 2, 0)),
        jnp.transpose(pair_block, (1, 0)),
        pair_count.reshape(1, SB),
        scalars=1,
        scratch=[pltpu.VMEM((3 * OB, LANES), F32)],
    )
    (terms,) = call(
        terms_kernel, (OB,), member, gathered, obs_value, obs_rinv, mix, scalars=1, unplaced=1
    )
    shares = swap(terms, "member")
    (windows,) = call(window_kernel, (4 * GRID,), shares)
    arrived = swap(windows.reshape(GRID, 1, 4 * LANES), "grid").reshape(4 * GRID, LANES)
    (combos,) = call(
        combine_kernel,
        (8 * 24,),
        arrived,
        mix,
        state_ens.reshape(SB * 4, LANES),
        scratch=[pltpu.VMEM((LANES, LANES), F32)],
    )
    matrices = swap(combos, "member")
    (update,) = call(transform_kernel, (SB * 4,), matrices)
    return swap(update.reshape(SB, 4, BV), "member")


def solution(mesh):
    return jax.shard_map(
        local,
        mesh=mesh,
        in_specs=(
            P("grid", "member", None),
            P("grid", "member", None),
            P("grid", None),
            P("grid", None),
            P("grid", None, None),
            P("grid", None),
            P("grid"),
        ),
        out_specs=P("grid", "member", None),
        check_vma=False,
    )
```
